128 devices in a mesh: scen: 4 (over x), path: 32 (over z, y, core).
Axes of the slice: x: 4, y: 4, z: 4, core: 2. Of those that a mesh axis runs over, the one named last changes fastest.
Arguments:
- states: float32 [4, 36, 8, 16384], P('scen', None, None, 'path'), may hold values from -1.5 to 1.5
- exercise_dates: int32 [4, 2], P('scen'), may hold values from 0 to 35, as said below
- itm_mask: int32 [4, 2, 16384], P('scen', None, 'path'), may hold values 0 or 1
- surrender: float32 [4, 36, 16384], P('scen', None, 'path'), may hold values from -0.5 to 1
- terminal: float32 [4, 16384], P('scen', 'path'), may hold values from -5 to 5
- discount: float32 [4, 2], P('scen'), may hold values from 0.5 to 1
- ls_table: int32 [256, 8], replicated, may hold values from 0 to 2, as said below
- proxy_table: int32 [2048, 8], replicated, may hold values from 0 to 2, as said below
Outputs:
- path_values: float32 [4, 16384], P('scen', 'path')
- coefficients: float32 [4, 2, 256], P('scen')
- proxy_gram: float32 [2048, 2048], P(('scen', 'path'))
- proxy_rhs: float32 [2048], P(('scen', 'path'))
The draws below stay inside these ranges and needn't reach their ends.
Inputs may be any that keep to these rules, and one draw needn't show every extreme that they name: `exercise_dates`: the first exercise date lies below 18 and the second at or above it. `ls_table`: no two rows are equal. `proxy_table`: no two rows are equal.
All inputs are finite; a program needn't handle non-finite values. No bound on the sum of `itm_mask` on one device may be relied on, other than what follows from the above.
Results may differ from the reference program's by a relative error of at most 0.005.
Values sent between devices are 32-bit elements; how exact they have to be, the bound alone decides.
A program may use at most 64 MiB of HBM per device.

```python
import math
import jax
import jax.numpy as jnp
from jax import lax

LS_TERMS = 256
PROXY_TERMS = 2048
STATE_VARS = 8
TGRID = 36
S_TOT = 4
NP = 16384
PROXY_ROWS = 65536


def draw_states(key, part):
    shape = (S_TOT, TGRID, STATE_VARS, NP)
    drawn = 0.8 * jax.random.normal(jax.random.fold_in(key, 5), shape, jnp.float32)
    return jnp.clip(drawn, -1.5, 1.5).astype(jnp.float32)


def draw_exercise_dates(key, part):
    first_key = jax.random.fold_in(key, 11)
    second_key = jax.random.fold_in(key, 23)
    early = jax.random.randint(first_key, (S_TOT, 1), 0, TGRID // 2)
    later = jax.random.randint(second_key, (S_TOT, 1), TGRID // 2, TGRID)
    return jnp.concatenate([early, later], axis=1).astype(jnp.int32)


def distinct_table(key, count):
    total = 3 ** STATE_VARS
    chosen = jax.random.permutation(key, jnp.arange(total, dtype=jnp.int32))[:count]
    powers = 3 ** jnp.arange(STATE_VARS, dtype=jnp.int32)
    return (chosen[:, None] // powers[None, :] % 3).astype(jnp.int32)


def draw_ls_table(key, part):
    return distinct_table(jax.random.fold_in(key, 37), LS_TERMS)


def draw_proxy_table(key, part):
    return distinct_table(jax.random.fold_in(key, 41), PROXY_TERMS)


def place_ends(values, own_key, smallest, top_value):
    place = [jax.random.randint(jax.random.fold_in(own_key, axis), (), 0, length) for axis, length in enumerate(values.shape)]
    widest = values.shape.index(max(values.shape))
    neighbour = place[:widest] + [(place[widest] + 1) % values.shape[widest]] + place[widest + 1:]
    return values.at[tuple(place)].set(smallest).at[tuple(neighbour)].set(top_value)


def block_scale(key, shape, shards, smallest, high):
    gain = 1.0
    for position, parts in shards:
        heights = jax.random.uniform(jax.random.fold_in(jax.random.fold_in(key, 6), position), (parts,), jnp.float32, smallest / len(shards), high / len(shards))
        gain = gain * jnp.repeat(jnp.exp(heights), shape[position] // parts).reshape((-1,) + (1,) * (len(shape) - 1 - position))
    return gain


def noise(rng, dims, width, limit, pieces=(), held_as=jnp.bfloat16):
    array = width * jax.random.normal(rng, dims, jnp.float32)
    if pieces:
        array = array * block_scale(rng, dims, pieces, -0.22, 0.18)
    return jnp.clip(array, -limit, limit).astype(held_as)


def setup_inputs(seed: int = 0) -> dict:
    arg_keys = jax.random.split(jax.random.key(seed), 9)
    return {
        "states": draw_states(jax.random.fold_in(arg_keys[8], 71), 0),
        "exercise_dates": draw_exercise_dates(jax.random.fold_in(arg_keys[8], 71), 0),
        "itm_mask": place_ends((jax.random.randint(arg_keys[2], (S_TOT, 2, NP), 0, 4) < 3).astype(jnp.int32), jax.random.fold_in(arg_keys[2], 1), 0, 1),
        "surrender": jnp.clip(-0.5 + 1.5 * jax.random.uniform(arg_keys[3], (S_TOT, TGRID, NP), jnp.float32) ** block_scale(arg_keys[3], (S_TOT, TGRID, NP), ((0, 4), (2, 32)), -0.2, 0.2), -0.5, 1.0),
        "terminal": noise(arg_keys[4], (S_TOT, NP), 1.0, 5.0, ((0, 4), (1, 32)), jnp.float32),
        "discount": jnp.clip(jnp.exp(math.log(1.0) - 0.6931472 * jax.random.uniform(arg_keys[5], (S_TOT, 2), jnp.float32) ** block_scale(arg_keys[5], (S_TOT, 2), ((0, 4),), -0.2, 0.2)), 0.5, 1.0),
        "ls_table": draw_ls_table(jax.random.fold_in(arg_keys[8], 71), 0),
        "proxy_table": draw_proxy_table(jax.random.fold_in(arg_keys[8], 71), 0),
    }


def hermite(current):
    return jnp.stack([jnp.ones_like(current), current, (current * current - 1.0) * 0.7071067811865476], axis=-2)

def basis_of(levels, table):
    result = jnp.take(levels[0], table[:, 0], axis=0)
    for column in range(1, table.shape[1]):
        result = result * jnp.take(levels[column], table[:, column], axis=0)
    return result

def scenario(states_one, dates_one, mask_one, surrender_one, terminal_one, discount_one, ls_table):
    values = terminal_one
    found = [None, None]
    for backward in (1, 0):
        moment = dates_one[backward]
        current = lax.dynamic_index_in_dim(states_one, moment, 0, keepdims=False)
        design = basis_of(hermite(current), ls_table).astype(jnp.bfloat16)
        values = discount_one[backward] * values
        live = mask_one[backward]
        weighted = design * live.astype(jnp.bfloat16)[None, :]
        gram = jnp.dot(weighted.astype(jnp.float32), design.T.astype(jnp.float32), preferred_element_type=jnp.float32)
        rhs = jnp.sum(weighted.astype(jnp.float32) * values[None, :], axis=1)
        system = gram / NP + 0.05 * jnp.eye(LS_TERMS, dtype=jnp.float32)
        factor = jnp.linalg.cholesky(system)
        coef = jax.scipy.linalg.cho_solve((factor, True), rhs / NP)
        found[backward] = coef
        continuation = jnp.dot(coef, design.astype(jnp.float32), precision=lax.Precision.HIGHEST)
        payoff = lax.dynamic_index_in_dim(surrender_one, moment, 0, keepdims=False)
        values = jnp.where(live > 0, jnp.maximum(payoff, continuation), values)
    return (values, jnp.stack(found, axis=0))

def reference(states, exercise_dates, itm_mask, surrender, terminal, discount, ls_table, proxy_table):

    def one(packed):
        return scenario(packed[0], packed[1], packed[2], packed[3], packed[4], packed[5], ls_table)
    path_values, coefficients = lax.map(one, (states, exercise_dates, itm_mask, surrender, terminal, discount))

    def accumulate(carry, packed):
        states_one, dates_one, values_one = packed
        current = lax.dynamic_index_in_dim(states_one, dates_one[0], 0, keepdims=False)
        proxy_design = basis_of(hermite(current), proxy_table).astype(jnp.bfloat16)
        gram_total = carry[0] + jnp.dot(proxy_design.astype(jnp.float32), proxy_design.T.astype(jnp.float32), preferred_element_type=jnp.float32)
        rhs_total = carry[1] + jnp.dot(proxy_design.astype(jnp.float32), values_one.astype(jnp.bfloat16).astype(jnp.float32), preferred_element_type=jnp.float32)
        return ((gram_total, rhs_total), None)
    start = (jnp.zeros((PROXY_TERMS, PROXY_TERMS), jnp.float32), jnp.zeros((PROXY_TERMS,), jnp.float32))
    totals, unused = lax.scan(accumulate, start, (states, exercise_dates, path_values))
    return (path_values, coefficients, totals[0] / PROXY_ROWS, totals[1] / PROXY_ROWS)
```

```python
import functools

import jax
import jax.numpy as jnp
from jax import lax
from jax.experimental import pallas as pl
from jax.experimental.pallas import tpu as pltpu
from jax.sharding import PartitionSpec as P

MESH = pl.DeviceIdType.MESH
HI = lax.Precision.HIGHEST
F32, BF16 = jnp.float32, jnp.bfloat16
ROOT_HALF = 0.7071067811865476
SIDE = 640
OWN = 5
PAIRS = 96
STEP = 32


def nt(a, b):
    return lax.dot_general(a, b, (((1,), (1,)), ((), ())), preferred_element_type=F32)


def nn(a, b):
    return jnp.dot(a, b, preferred_element_type=F32)


def halves(x):
    high = x.astype(BF16)
    return high, (x - high.astype(F32)).astype(BF16)


def three_rows(x):
    high = x.astype(BF16).astype(F32)
    rest = x - high
    mid = rest.astype(BF16).astype(F32)
    sub = lax.broadcasted_iota(jnp.int32, (8, x.shape[1]), 0)
    low = rest - mid
    return jnp.where(
        sub == 0, high, jnp.where(sub == 1, mid, jnp.where(sub == 2, low, 0.0))
    ).astype(BF16)


def add_rows(x):
    return x[0:1] + x[1:2] + x[2:3]


def products(factors, pair_a, pair_b, out, levels):
    count = levels * levels
    for i in range(levels):
        for j in range(levels):
            row = i * levels + j
            pair_a[row : row + 1, :] = factors[0][i] * factors[1][j]
            pair_b[row : row + 1, :] = factors[2][i] * factors[3][j]
    for i in range(count):
        out[i * count : (i + 1) * count, :] = pair_a[i : i + 1, :] * pair_b[0:count, :]


def local_kernel(
    dates, disc, early, late, mask, terminal, table, design_out, gram_out, rhs_out, moment_out,
    pair_a, pair_b, left, right, whole,
):
    paths = terminal.shape[1]
    for backward, block in ((0, early), (1, late)):
        u = block[0, 0]
        h = (u * u - 1.0) * ROOT_HALF
        for top in range(0, table.shape[0], 32):
            t = table[top : top + 32, :]
            result = None
            for v in range(8):
                degree = jnp.broadcast_to(t[:, v : v + 1], (32, paths))
                level = jnp.where(
                    degree == 1, u[v : v + 1, :], jnp.where(degree == 2, h[v : v + 1, :], 1.0)
                )
                result = level if result is None else result * level
            design_out[backward, top : top + 32, :] = result.astype(BF16)
        design = design_out[backward]
        weighted = design * mask[backward : backward + 1, :].astype(F32).astype(BF16)
        gram = nt(weighted, design)
        gram_out[backward, 0:128, :] = gram[0:128, 0:128]
        gram_out[backward, 128:256, :] = gram[128:256, 0:128]
        gram_out[backward, 256:384, :] = gram[128:256, 128:256]
        if backward == 1:
            values = disc[1] * terminal[...]
            rhs_out[...] = add_rows(nt(three_rows(values), weighted))
    u = early[0, 0]
    g = u * u - 1.0
    one = jnp.ones((1, paths), F32)
    def levels(v):
        x, y = u[v : v + 1, :], g[v : v + 1, :]
        return [one, x, y, x * y, y * y]
    for side, first in ((left, 0), (right, 4)):
        side[624:SIDE, :] = jnp.zeros((SIDE - 624, paths), F32)
        products([levels(first + v) for v in range(4)], pair_a, pair_b, side, 5)
    lh, ll = halves(left[...])
    rh, rl = halves(right[...])
    whole[...] = nt(lh, rh) + nt(lh, rl) + nt(ll, rh)
    for b in range(SIDE // OWN):
        moment_out[b] = whole[b * OWN : (b + 1) * OWN, :]


def exchange_kernel(
    paths, scens, ls, rhs, mom, ls_out, rhs_out, mom_out,
    ls_in, rhs_in, mom_half, mom_acc, mom_in,
    ls_s, ls_r, rhs_s, rhs_r, ag_s, ag_r, half_s, half_r, mom_s, mom_r,
):
    s, p = lax.axis_index("scen"), lax.axis_index("path")
    core, seat = p % 2, p // 2
    seats = paths // 2
    group = scens * seats
    me = s * seats + seat

    def path_peer(d):
        return (p + d) % paths

    def core_peer(d):
        return (me + d) % group

    def core_id(j):
        return (j // seats, (j % seats) * 2 + core)

    barrier = pltpu.get_barrier_semaphore()

    @pl.loop(1, paths)
    def _(d):
        pl.semaphore_signal(barrier, inc=1, device_id=(s, path_peer(d)), device_id_type=MESH)

    @pl.loop(1, group)
    def _(d):
        pl.semaphore_signal(barrier, inc=1, device_id=core_id(core_peer(d)), device_id_type=MESH)

    pl.semaphore_wait(barrier, paths - 1 + group - 1)

    def half_copy():
        return pltpu.make_async_remote_copy(
            src_ref=mom.at[1 - core], dst_ref=mom_half, send_sem=half_s, recv_sem=half_r,
            device_id=(s, seat * 2 + 1 - core), device_id_type=MESH)

    def ls_copy(q):
        return pltpu.make_async_remote_copy(
            src_ref=ls.at[q], dst_ref=ls_in.at[p], send_sem=ls_s.at[q], recv_sem=ls_r.at[p],
            device_id=(s, q), device_id_type=MESH)

    def rhs_copy(q):
        return pltpu.make_async_remote_copy(
            src_ref=rhs, dst_ref=rhs_in.at[p], send_sem=rhs_s.at[q], recv_sem=rhs_r.at[p],
            device_id=(s, q), device_id_type=MESH)

    def ag_copy(q):
        return pltpu.make_async_remote_copy(
            src_ref=ls_out.at[p], dst_ref=ls_out.at[p], send_sem=ag_s.at[q], recv_sem=ag_r.at[p],
            device_id=(s, q), device_id_type=MESH)

    def mom_copy(j):
        return pltpu.make_async_remote_copy(
            src_ref=mom_acc.at[j], dst_ref=mom_in.at[me], send_sem=mom_s.at[j], recv_sem=mom_r.at[me],
            device_id=core_id(j), device_id_type=MESH)

    def arrived(buffer, sems, slot):
        pltpu.make_async_copy(buffer.at[slot], buffer.at[slot], sems.at[slot]).wait()

    half_copy().start()

    @pl.loop(1, paths)
    def _(d):
        ls_copy(path_peer(d)).start()
        rhs_copy(path_peer(d)).start()

    @pl.loop(1, paths)
    def _(d):
        arrived(ls_in, ls_r, path_peer(d))
        arrived(rhs_in, rhs_r, path_peer(d))

    def add_ls(d, carry):
        return carry[0] + ls_in[path_peer(d)], carry[1] + rhs_in[path_peer(d)]

    total, rhs_total = lax.fori_loop(1, paths, add_ls, (ls[p], rhs[...]))
    ls_out[p] = total
    rhs_out[...] = rhs_total

    @pl.loop(1, paths)
    def _(d):
        ag_copy(path_peer(d)).start()

    half_copy().wait()

    @pl.loop(0, group)
    def _(j):
        mom_acc[j] = mom[core, j] + mom_half[j]

    @pl.loop(1, group)
    def _(d):
        mom_copy(core_peer(d)).start()

    @pl.loop(1, paths)
    def _(d):
        arrived(ls_out, ag_r, path_peer(d))

    @pl.loop(1, group)
    def _(d):
        arrived(mom_in, mom_r, core_peer(d))

    def add_mom(d, carry):
        return carry + mom_in[core_peer(d)]

    mom_out[...] = lax.fori_loop(1, group, add_mom, mom_acc[me])

    @pl.loop(1, paths)
    def _(d):
        ls_copy(path_peer(d)).wait_send()
        rhs_copy(path_peer(d)).wait_send()
        ag_copy(path_peer(d)).wait_send()

    @pl.loop(1, group)
    def _(d):
        mom_copy(core_peer(d)).wait_send()


def second_kernel(
    paths, scens, rhs, mom, rhs_out, full, rhs_in,
    own_s, rhs_s, rhs_r, mom_s, mom_r, half_s, half_r,
):
    s, p = lax.axis_index("scen"), lax.axis_index("path")
    core, seat = p % 2, p // 2
    seats = paths // 2
    group = scens * seats
    me = s * seats + seat

    def path_peer(d):
        return (p + d) % paths

    def core_peer(d):
        return (me + d) % group

    def core_id(j):
        return (j // seats, (j % seats) * 2 + core)

    barrier = pltpu.get_barrier_semaphore()

    @pl.loop(1, paths)
    def _(d):
        pl.semaphore_signal(barrier, inc=1, device_id=(s, path_peer(d)), device_id_type=MESH)

    @pl.loop(1, group)
    def _(d):
        pl.semaphore_signal(barrier, inc=1, device_id=core_id(core_peer(d)), device_id_type=MESH)

    pl.semaphore_wait(barrier, paths - 1 + group - 1)

    def rhs_copy(q):
        return pltpu.make_async_remote_copy(
            src_ref=rhs, dst_ref=rhs_in.at[p], send_sem=rhs_s.at[q], recv_sem=rhs_r.at[p],
            device_id=(s, q), device_id_type=MESH)

    def mom_copy(j):
        return pltpu.make_async_remote_copy(
            src_ref=mom, dst_ref=full.at[core, me], send_sem=mom_s.at[j], recv_sem=mom_r.at[me],
            device_id=core_id(j), device_id_type=MESH)

    def half_copy():
        return pltpu.make_async_remote_copy(
            src_ref=full.at[core], dst_ref=full.at[core], send_sem=half_s, recv_sem=half_r,
            device_id=(s, seat * 2 + 1 - core), device_id_type=MESH)

    @pl.loop(1, paths)
    def _(d):
        rhs_copy(path_peer(d)).start()

    @pl.loop(1, group)
    def _(d):
        mom_copy(core_peer(d)).start()

    own = pltpu.make_async_copy(mom, full.at[core, me], own_s)
    own.start()

    @pl.loop(1, paths)
    def _(d):
        slot = path_peer(d)
        pltpu.make_async_copy(rhs_in.at[slot], rhs_in.at[slot], rhs_r.at[slot]).wait()

    def add_rhs(d, carry):
        return carry + rhs_in[path_peer(d)]

    rhs_out[...] = lax.fori_loop(1, paths, add_rhs, rhs[...])
    own.wait()

    @pl.loop(1, group)
    def _(d):
        slot = core_peer(d)
        pltpu.make_async_copy(full.at[core, slot], full.at[core, slot], mom_r.at[slot]).wait()

    half_copy().start()
    half_copy().wait()

    @pl.loop(1, paths)
    def _(d):
        rhs_copy(path_peer(d)).wait_send()

    @pl.loop(1, group)
    def _(d):
        mom_copy(core_peer(d)).wait_send()


def third_kernel(paths, scens, parts, out, parts_in, mine, mine_in, a_s, a_r, b_s, b_r):
    s, p = lax.axis_index("scen"), lax.axis_index("path")

    def path_peer(d):
        return (p + d) % paths

    def scen_peer(d):
        return (s + d) % scens

    barrier = pltpu.get_barrier_semaphore()

    @pl.loop(1, paths)
    def _(d):
        pl.semaphore_signal(barrier, inc=1, device_id=(s, path_peer(d)), device_id_type=MESH)

    @pl.loop(1, scens)
    def _(d):
        pl.semaphore_signal(barrier, inc=1, device_id=(scen_peer(d), p), device_id_type=MESH)

    pl.semaphore_wait(barrier, paths - 1 + scens - 1)

    def a_copy(q):
        return pltpu.make_async_remote_copy(
            src_ref=parts.at[q], dst_ref=parts_in.at[p], send_sem=a_s.at[q], recv_sem=a_r.at[p],
            device_id=(s, q), device_id_type=MESH)

    def b_copy(t):
        return pltpu.make_async_remote_copy(
            src_ref=mine.at[t], dst_ref=mine_in.at[s], send_sem=b_s.at[t], recv_sem=b_r.at[s],
            device_id=(t, p), device_id_type=MESH)

    @pl.loop(1, paths)
    def _(d):
        a_copy(path_peer(d)).start()

    @pl.loop(1, paths)
    def _(d):
        slot = path_peer(d)
        pltpu.make_async_copy(parts_in.at[slot], parts_in.at[slot], a_r.at[slot]).wait()

    def add_a(d, carry):
        return carry + parts_in[path_peer(d)]

    mine[...] = lax.fori_loop(1, paths, add_a, parts[p])

    @pl.loop(1, scens)
    def _(d):
        b_copy(scen_peer(d)).start()

    @pl.loop(1, scens)
    def _(d):
        slot = scen_peer(d)
        pltpu.make_async_copy(mine_in.at[slot], mine_in.at[slot], b_r.at[slot]).wait()

    def add_b(d, carry):
        return carry + mine_in[scen_peer(d)]

    out[...] = lax.fori_loop(1, scens, add_b, mine[s])

    @pl.loop(1, paths)
    def _(d):
        a_copy(path_peer(d)).wait_send()

    @pl.loop(1, scens)
    def _(d):
        b_copy(scen_peer(d)).wait_send()


def sweep_small(e, n):
    def at(i, j):
        return e[min(i, j), max(i, j)]

    for k in range(0, n, 2):
        p, q, s = e[k, k], e[k, k + 1], e[k + 1, k + 1]
        w = 1.0 / (p * s - q * q)
        pw, qw, sw = p * w, q * w, s * w
        others = [i for i in range(n) if i not in (k, k + 1)]
        r0 = {i: at(k, i) for i in others}
        r1 = {i: at(k + 1, i) for i in others}
        x0 = {i: sw * r0[i] - qw * r1[i] for i in others}
        x1 = {i: pw * r1[i] - qw * r0[i] for i in others}
        for i in others:
            for j in others:
                if i <= j:
                    e[i, j] = e[i, j] - (r0[i] * x0[j] + r1[i] * x1[j])
        for i in others:
            e[min(i, k), max(i, k)] = x0[i]
            e[min(i, k + 1), max(i, k + 1)] = x1[i]
        e[k, k], e[k, k + 1], e[k + 1, k + 1] = -sw, qw, -pw
    return e


def tree_sum(terms):
    while len(terms) > 1:
        terms = [terms[t] + terms[t + 1] for t in range(0, len(terms), 2)]
    return terms[0]


def leaf(a, e_ref, r_ref):
    lane = lax.broadcasted_iota(jnp.int32, (STEP, 128), 1)
    lane8 = lax.broadcasted_iota(jnp.int32, (8, 128), 1)
    sub8 = lax.broadcasted_iota(jnp.int32, (8, 128), 0)
    half = lane - lane % 64
    in_half = lane8 % 64
    for o in range(0, STEP, 8):
        cols = [jnp.take_along_axis(a, half + (o + j), axis=1) for j in range(8)]
        r_ref[...] = a[o : o + 8, :]
        for j in range(8):
            e_ref[j] = cols[j][o : o + 8, :]
        e = {(i, j): e_ref[j, pl.ds(i, 8, stride=0), :] for i in range(8) for j in range(i, 8)}
        e = sweep_small(e, 8)
        rows = [r_ref[pl.ds(i, 8, stride=0), :] for i in range(8)]
        xs = []
        for i in range(8):
            entries = [e[min(i, j), max(i, j)] for j in range(8)]
            x = -tree_sum([entries[j] * rows[j] for j in range(8)])
            for j in range(8):
                x = jnp.where(in_half == o + j, entries[j], x)
            xs.append(x)
        tile = xs[0]
        for i in range(1, 8):
            tile = jnp.where(sub8 == i, xs[i], tile)
        inside = (in_half >= o) & (in_half < o + 8)
        tiles = []
        for t in range(0, STEP, 8):
            if t == o:
                tiles.append(tile)
            else:
                base = jnp.where(inside, 0.0, a[t : t + 8, :])
                tiles.append(base - tree_sum([cols[j][t : t + 8, :] * xs[j] for j in range(8)]))
        a = jnp.concatenate(tiles, axis=0)
    return a


def invert(a_ref, e_ref, r_ref):
    n = a_ref.shape[1]
    lane = lax.broadcasted_iota(jnp.int32, (STEP, n), 1)
    lane1 = lax.broadcasted_iota(jnp.int32, (STEP, 128), 1)
    lane2 = lax.broadcasted_iota(jnp.int32, (n - STEP, n), 1)

    def body(k, _):
        first = [a_ref[d, 0:STEP, 0:128] for d in range(2)]
        both = leaf(jnp.where(lane1 < 64, first[0], pltpu.roll(first[1], 64, 1)), e_ref, r_ref)
        for d, neg in enumerate((both, pltpu.roll(both, 64, 1))):
            r = a_ref[d, 0:STEP, :]
            rest = a_ref[d, STEP:, :]
            x = jnp.dot(neg[:, 0:STEP], r, precision=HI, preferred_element_type=F32)
            xt = jnp.where(lane < STEP, jnp.concatenate([neg, neg], axis=1), -x)
            new = jnp.where(lane2 < STEP, 0.0, rest) - jnp.dot(
                rest[:, 0:STEP], xt, precision=HI, preferred_element_type=F32
            )
            a_ref[d, 0 : n - STEP, :] = pltpu.roll(new, n - STEP, 1)
            a_ref[d, n - STEP :, :] = pltpu.roll(xt, n - STEP, 1)
        return 0

    lax.fori_loop(0, n // STEP, body, 0)


def solve_kernel(
    total, dates, disc, gram, rhs, design, mask, surrender, terminal,
    coef_out, inv_out, values_out, rhs_out, a_ref, e_ref, r_ref,
):
    n = a_ref.shape[1]
    scale = 1.0 / total
    ri = lax.broadcasted_iota(jnp.int32, (128, 128), 0)
    ci = lax.broadcasted_iota(jnp.int32, (128, 128), 1)
    ridge = jnp.where(ri == ci, 0.05, 0.0)
    for d in range(2):
        corner = gram[d, 128:256, :] * scale
        a_ref[d, 0:128, 0:128] = gram[d, 0:128, :] * scale + ridge
        a_ref[d, 128:256, 0:128] = corner
        a_ref[d, 0:128, 128:256] = corner.T
        a_ref[d, 128:256, 128:256] = gram[d, 256:384, :] * scale + ridge
    invert(a_ref, e_ref, r_ref)
    inv_out[...] = -a_ref[0]
    side = jnp.broadcast_to(rhs[...] * scale, (8, n))
    coef = -jnp.dot(side, a_ref[1], precision=HI, preferred_element_type=F32)
    coef_out[...] = coef[0:1]
    continuation = add_rows(nn(three_rows(coef[0:1]), design[1]))
    payoff = surrender[pl.ds(dates[1], 1), :]
    values = disc[1] * terminal[...]
    values = jnp.where(mask[1:2, :] > 0, jnp.maximum(payoff, continuation), values)
    values = disc[0] * values
    values_out[...] = values
    weighted = design[0] * mask[0:1, :].astype(F32).astype(BF16)
    rhs_out[...] = add_rows(nt(three_rows(values), weighted))


def one_hots(table_t, low_out, high_out):
    row = lax.broadcasted_iota(jnp.int32, low_out.shape, 0)
    for first, out in ((0, low_out), (4, high_out)):
        t = [table_t[first + v : first + v + 1, :] for v in range(4)]
        code = ((t[0] * 3 + t[1]) * 3 + t[2]) * 3 + t[3]
        out[...] = jnp.where(row == code, 1.0, 0.0).astype(out.dtype)


def tail_kernel(
    total, dates, inv, rhs, design, mask, surrender, values, early, table_t,
    values_out, coef_out, rhs_out, pair_a, pair_b, left, right, low, high,
):
    n = inv.shape[0]
    paths = values.shape[1]
    side = jnp.broadcast_to(rhs[...] * (1.0 / total), (8, n))
    coef = jnp.dot(side, inv[...], precision=HI, preferred_element_type=F32)[0:1]
    coef_out[...] = coef
    continuation = add_rows(nn(three_rows(coef), design[0]))
    payoff = surrender[pl.ds(dates[0], 1), :]
    final = jnp.where(mask[0:1, :] > 0, jnp.maximum(payoff, continuation), values[...])
    values_out[...] = final
    u = early[0, 0]
    h = (u * u - 1.0) * ROOT_HALF
    one = jnp.ones((1, paths), F32)
    for out, first in ((left, 0), (right, 4)):
        out[80:PAIRS, :] = jnp.zeros((PAIRS - 80, paths), F32)
        levels = [[one, u[first + v : first + v + 1, :], h[first + v : first + v + 1, :]] for v in range(4)]
        products(levels, pair_a, pair_b, out, 3)
    rounded = final.astype(BF16).astype(F32)
    lh, ll = halves(left[...] * rounded)
    rh, rl = halves(right[...])
    one_hots(table_t, low, high)
    wh, wl = halves(nt(rh, lh) + nt(rh, ll) + nt(rl, lh))
    picked = (nn(wh, low[...]) + nn(wl, low[...])) * high[...]
    rhs_out[...] = jnp.sum(picked, axis=0, keepdims=True)


def gram_kernel(total, mine, full, table_t, out, whole, both, pattern, pick_l, pick_r, low, high):
    row = lax.broadcasted_iota(jnp.int32, (PAIRS, 1), 0)
    lane = lax.broadcasted_iota(jnp.int32, (1, SIDE), 1)
    for v, (three, five) in enumerate(((27, 125), (9, 25), (3, 5), (1, 1))):
        b = jnp.where(row < 81, (row // three) % 3, -9)
        m = jnp.where(lane < 625, (lane // five) % 5, -20)
        b, m = jnp.broadcast_to(b, (PAIRS, SIDE)), jnp.broadcast_to(m, (PAIRS, SIDE))
        ones = ((b == 0) & (m == 1)) | ((b == 1) & ((m == 0) | (m == 2))) | ((b == 2) & (m == 3))
        pattern[v, 0] = jnp.where(m == b, 1.0, 0.0).astype(BF16)
        pattern[v, 1] = jnp.where(ones, 1.0, 0.0).astype(BF16)
        pattern[v, 2] = jnp.where(m == b + 2, 1.0, 0.0).astype(BF16)
    for b in range(SIDE // OWN):
        whole[b * OWN : (b + 1) * OWN, :] = full[b]
    mh, ml = halves(whole[...])
    both[0] = mh
    both[1] = ml
    one_hots(table_t, low, high)
    scale = None
    for v in range(8):
        factor = jnp.where(table_t[v : v + 1, :] == 2, ROOT_HALF, 1.0)
        scale = factor if scale is None else scale * factor

    @pl.loop(0, out.shape[0])
    def _(r):
        def pattern_of(first):
            result = None
            for v in range(4):
                block = pattern[v, mine[r * 8 + first + v]]
                result = block if result is None else result * block
            return result

        own = 1.0 / total
        for v in range(8):
            own = own * jnp.where(mine[r * 8 + v] == 2, ROOT_HALF, 1.0)
        pick_l[...] = pattern_of(0)
        pick_r[...] = pattern_of(4)
        yh, yl = halves(nn(pick_l[...], both[0]) + nn(pick_l[...], both[1]))
        zh, zl = halves(nt(pick_r[...], yh) + nt(pick_r[...], yl))
        picked = (nn(zh, low[...]) + nn(zl, low[...])) * high[...]
        out[pl.ds(r, 1), :] = jnp.sum(picked, axis=0, keepdims=True) * scale * own


VMEM = pl.BlockSpec(memory_space=pltpu.VMEM)
SMEM = pl.BlockSpec(memory_space=pltpu.SMEM)
DMA = pltpu.SemaphoreType.DMA


def on_device(
    states, exercise_dates, itm_mask, surrender, terminal, discount, ls_table, proxy_table
):
    scens, path_devices = lax.axis_size("scen"), lax.axis_size("path")
    paths = states.shape[3]
    terms, proxy_terms = ls_table.shape[0], proxy_table.shape[0]
    devices = scens * path_devices
    total_paths = paths * path_devices
    total_rows = total_paths * scens
    dates, disc = exercise_dates[0], discount[0]
    mask, payoffs = itm_mask[0], surrender[0]
    table_t = proxy_table.T
    own_rows = proxy_terms // devices
    index = lax.axis_index("scen") * path_devices + lax.axis_index("path")
    mine = lax.dynamic_slice(proxy_table, (index * own_rows, 0), (own_rows, 8)).reshape(-1)

    def state_spec(j):
        return pl.BlockSpec((1, 1, 8, paths), lambda i, d: (0, d[j], 0, 0))

    early_spec = state_spec(0)
    design, gram, rhs, moments = pl.pallas_call(
        local_kernel,
        grid_spec=pltpu.PrefetchScalarGridSpec(
            num_scalar_prefetch=1,
            grid=(1,),
            in_specs=[SMEM, early_spec, state_spec(1), VMEM, VMEM, VMEM],
            out_specs=[VMEM] * 4,
            scratch_shapes=[
                pltpu.VMEM((32, paths), F32),
                pltpu.VMEM((32, paths), F32),
                pltpu.VMEM((SIDE, paths), F32),
                pltpu.VMEM((SIDE, paths), F32),
                pltpu.VMEM((SIDE, SIDE), F32),
            ],
        ),
        out_shape=(
            jax.ShapeDtypeStruct((2, terms, paths), BF16),
            jax.ShapeDtypeStruct((2, 384, 128), F32),
            jax.ShapeDtypeStruct((1, terms), F32),
            jax.ShapeDtypeStruct((devices, OWN, SIDE), F32),
        ),
        name="local",
    )(dates, disc, states, states, mask, terminal, ls_table)

    half = devices // 2
    rows = 768 // path_devices
    gram, rhs, block = pl.pallas_call(
        functools.partial(exchange_kernel, path_devices, scens),
        out_shape=(
            jax.ShapeDtypeStruct((path_devices, rows, 128), F32),
            jax.ShapeDtypeStruct((1, terms), F32),
            jax.ShapeDtypeStruct((OWN, SIDE), F32),
        ),
        in_specs=[VMEM] * 3,
        out_specs=[VMEM] * 3,
        scratch_shapes=[
            pltpu.VMEM((path_devices, rows, 128), F32),
            pltpu.VMEM((path_devices, 1, terms), F32),
            pltpu.VMEM((half, OWN, SIDE), F32),
            pltpu.VMEM((half, OWN, SIDE), F32),
            pltpu.VMEM((half, OWN, SIDE), F32),
            DMA((path_devices,)), DMA((path_devices,)),
            DMA((path_devices,)), DMA((path_devices,)),
            DMA((path_devices,)), DMA((path_devices,)),
            DMA, DMA,
            DMA((half,)), DMA((half,)),
        ],
        compiler_params=pltpu.CompilerParams(collective_id=0, has_side_effects=True),
        name="exchange",
    )(gram.reshape(path_devices, rows, 128), rhs, moments.reshape(2, half, OWN, SIDE))

    coef_late, inv, values, rhs = pl.pallas_call(
        functools.partial(solve_kernel, total_paths),
        out_shape=(
            jax.ShapeDtypeStruct((1, terms), F32),
            jax.ShapeDtypeStruct((terms, terms), F32),
            jax.ShapeDtypeStruct((1, paths), F32),
            jax.ShapeDtypeStruct((1, terms), F32),
        ),
        in_specs=[SMEM, SMEM] + [VMEM] * 6,
        out_specs=[VMEM] * 4,
        scratch_shapes=[
            pltpu.VMEM((2, terms, terms), F32),
            pltpu.VMEM((8, 8, 128), F32),
            pltpu.VMEM((8, 128), F32),
        ],
        name="solve",
    )(dates, disc, gram.reshape(2, 384, 128), rhs, design, mask, payoffs, terminal)

    rhs, full = pl.pallas_call(
        functools.partial(second_kernel, path_devices, scens),
        out_shape=(
            jax.ShapeDtypeStruct((1, terms), F32),
            jax.ShapeDtypeStruct((2, half, OWN, SIDE), F32),
        ),
        in_specs=[VMEM] * 2,
        out_specs=[VMEM] * 2,
        scratch_shapes=[
            pltpu.VMEM((path_devices, 1, terms), F32),
            DMA,
            DMA((path_devices,)), DMA((path_devices,)),
            DMA((half,)), DMA((half,)),
            DMA, DMA,
        ],
        compiler_params=pltpu.CompilerParams(collective_id=1, has_side_effects=True),
        name="second",
    )(rhs, block)

    values, coef_early, proxy_part = pl.pallas_call(
        functools.partial(tail_kernel, total_paths),
        grid_spec=pltpu.PrefetchScalarGridSpec(
            num_scalar_prefetch=1,
            grid=(1,),
            in_specs=[VMEM] * 6 + [early_spec, VMEM],
            out_specs=[VMEM] * 3,
            scratch_shapes=[
                pltpu.VMEM((16, paths), F32),
                pltpu.VMEM((16, paths), F32),
                pltpu.VMEM((PAIRS, paths), F32),
                pltpu.VMEM((PAIRS, paths), F32),
                pltpu.VMEM((PAIRS, proxy_terms), BF16),
                pltpu.VMEM((PAIRS, proxy_terms), F32),
            ],
        ),
        out_shape=(
            jax.ShapeDtypeStruct((1, paths), F32),
            jax.ShapeDtypeStruct((1, terms), F32),
            jax.ShapeDtypeStruct((1, proxy_terms), F32),
        ),
        name="tail",
    )(dates, inv, rhs, design, mask, payoffs, values, states, table_t)

    parts = proxy_part.reshape(scens, path_devices, 1, own_rows).transpose(1, 0, 2, 3)
    parts = jnp.pad(parts, ((0, 0), (0, 0), (0, 0), (0, 128 - own_rows)))
    proxy_rhs = pl.pallas_call(
        functools.partial(third_kernel, path_devices, scens),
        out_shape=jax.ShapeDtypeStruct((1, 128), F32),
        in_specs=[VMEM],
        out_specs=VMEM,
        scratch_shapes=[
            pltpu.VMEM((path_devices, scens, 1, 128), F32),
            pltpu.VMEM((scens, 1, 128), F32),
            pltpu.VMEM((scens, 1, 128), F32),
            DMA((path_devices,)), DMA((path_devices,)),
            DMA((scens,)), DMA((scens,)),
        ],
        compiler_params=pltpu.CompilerParams(collective_id=2, has_side_effects=True),
        name="third",
    )(parts)

    proxy_gram = pl.pallas_call(
        functools.partial(gram_kernel, total_rows),
        grid_spec=pltpu.PrefetchScalarGridSpec(
            num_scalar_prefetch=1,
            grid=(1,),
            in_specs=[VMEM] * 2,
            out_specs=VMEM,
            scratch_shapes=[
                pltpu.VMEM((SIDE, SIDE), F32),
                pltpu.VMEM((2, SIDE, SIDE), BF16),
                pltpu.VMEM((4, 3, PAIRS, SIDE), BF16),
                pltpu.VMEM((PAIRS, SIDE), BF16),
                pltpu.VMEM((PAIRS, SIDE), BF16),
                pltpu.VMEM((PAIRS, proxy_terms), BF16),
                pltpu.VMEM((PAIRS, proxy_terms), F32),
            ],
        ),
        out_shape=jax.ShapeDtypeStruct((own_rows, proxy_terms), F32),
        name="gram",
    )(mine, full.reshape(devices, OWN, SIDE), table_t)

    coefficients = jnp.stack([coef_early, coef_late], axis=1)
    return (values, coefficients, proxy_gram, proxy_rhs[0, :own_rows] * (1.0 / total_rows))


def solution(mesh):
    placed = (
        P("scen", None, None, "path"),
        P("scen", None),
        P("scen", None, "path"),
        P("scen", None, "path"),
        P("scen", "path"),
        P("scen", None),
        P(),
        P(),
    )
    return jax.shard_map(
        on_device,
        mesh=mesh,
        in_specs=placed,
        out_specs=(
            P("scen", "path"),
            P("scen", None, None),
            P(("scen", "path"), None),
            P(("scen", "path")),
        ),
        check_vma=False,
    )
```

```python
import functools

import jax
import jax.numpy as jnp
from jax import lax
from jax.experimental import pallas as pl
from jax.experimental.pallas import tpu as pltpu
from jax.sharding import PartitionSpec as P

MESH = pl.DeviceIdType.MESH
HI = lax.Precision.HIGHEST
F32, BF16 = jnp.float32, jnp.bfloat16
ROOT_HALF = 0.7071067811865476
SIDE = 640
CHUNK = 400
PAIRS = 96
STEP = 32


def nt(a, b):
    return lax.dot_general(a, b, (((1,), (1,)), ((), ())), preferred_element_type=F32)


def nn(a, b):
    return jnp.dot(a, b, preferred_element_type=F32)


def halves(x):
    high = x.astype(BF16)
    return high, (x - high.astype(F32)).astype(BF16)


def three_rows(x):
    high = x.astype(BF16).astype(F32)
    rest = x - high
    mid = rest.astype(BF16).astype(F32)
    sub = lax.broadcasted_iota(jnp.int32, (8, x.shape[1]), 0)
    low = rest - mid
    return jnp.where(
        sub == 0, high, jnp.where(sub == 1, mid, jnp.where(sub == 2, low, 0.0))
    ).astype(BF16)


def add_rows(x):
    return x[0:1] + x[1:2] + x[2:3]


def products(factors, pair_a, pair_b, out, levels):
    count = levels * levels
    for i in range(levels):
        for j in range(levels):
            row = i * levels + j
            pair_a[row : row + 1, :] = factors[0][i] * factors[1][j]
            pair_b[row : row + 1, :] = factors[2][i] * factors[3][j]
    for i in range(count):
        out[i * count : (i + 1) * count, :] = pair_a[i : i + 1, :] * pair_b[0:count, :]


def sweep_small(e, n):
    def at(i, j):
        return e[min(i, j), max(i, j)]

    for k in range(0, n, 2):
        p, q, s = e[k, k], e[k, k + 1], e[k + 1, k + 1]
        w = 1.0 / (p * s - q * q)
        pw, qw, sw = p * w, q * w, s * w
        others = [i for i in range(n) if i not in (k, k + 1)]
        r0 = {i: at(k, i) for i in others}
        r1 = {i: at(k + 1, i) for i in others}
        x0 = {i: sw * r0[i] - qw * r1[i] for i in others}
        x1 = {i: pw * r1[i] - qw * r0[i] for i in others}
        for i in others:
            for j in others:
                if i <= j:
                    e[i, j] = e[i, j] - (r0[i] * x0[j] + r1[i] * x1[j])
        for i in others:
            e[min(i, k), max(i, k)] = x0[i]
            e[min(i, k + 1), max(i, k + 1)] = x1[i]
        e[k, k], e[k, k + 1], e[k + 1, k + 1] = -sw, qw, -pw
    return e


def tree_sum(terms):
    while len(terms) > 1:
        terms = [terms[t] + terms[t + 1] for t in range(0, len(terms), 2)]
    return terms[0]


def leaf(a, e_ref, r_ref):
    lane = lax.broadcasted_iota(jnp.int32, (STEP, 128), 1)
    lane8 = lax.broadcasted_iota(jnp.int32, (8, 128), 1)
    sub8 = lax.broadcasted_iota(jnp.int32, (8, 128), 0)
    half = lane - lane % 64
    in_half = lane8 % 64
    for o in range(0, STEP, 8):
        cols = [jnp.take_along_axis(a, half + (o + j), axis=1) for j in range(8)]
        r_ref[...] = a[o : o + 8, :]
        for j in range(8):
            e_ref[j] = cols[j][o : o + 8, :]
        e = {(i, j): e_ref[j, pl.ds(i, 8, stride=0), :] for i in range(8) for j in range(i, 8)}
        e = sweep_small(e, 8)
        rows = [r_ref[pl.ds(i, 8, stride=0), :] for i in range(8)]
        xs = []
        for i in range(8):
            entries = [e[min(i, j), max(i, j)] for j in range(8)]
            x = -tree_sum([entries[j] * rows[j] for j in range(8)])
            for j in range(8):
                x = jnp.where(in_half == o + j, entries[j], x)
            xs.append(x)
        tile = xs[0]
        for i in range(1, 8):
            tile = jnp.where(sub8 == i, xs[i], tile)
        inside = (in_half >= o) & (in_half < o + 8)
        tiles = []
        for t in range(0, STEP, 8):
            if t == o:
                tiles.append(tile)
            else:
                base = jnp.where(inside, 0.0, a[t : t + 8, :])
                tiles.append(base - tree_sum([cols[j][t : t + 8, :] * xs[j] for j in range(8)]))
        a = jnp.concatenate(tiles, axis=0)
    return a


def eliminate(a_ref, e_ref, r_ref, start, stop):
    n = a_ref.shape[1]
    lane = lax.broadcasted_iota(jnp.int32, (STEP, n), 1)
    lane1 = lax.broadcasted_iota(jnp.int32, (STEP, 128), 1)
    lane2 = lax.broadcasted_iota(jnp.int32, (n - STEP, n), 1)

    def body(k, _):
        first = [a_ref[d, 0:STEP, 0:128] for d in range(2)]
        both = leaf(jnp.where(lane1 < 64, first[0], pltpu.roll(first[1], 64, 1)), e_ref, r_ref)
        for d, neg in enumerate((both, pltpu.roll(both, 64, 1))):
            r = a_ref[d, 0:STEP, :]
            rest = a_ref[d, STEP:, :]
            x = jnp.dot(neg[:, 0:STEP], r, precision=HI, preferred_element_type=F32)
            xt = jnp.where(lane < STEP, jnp.concatenate([neg, neg], axis=1), -x)
            new = jnp.where(lane2 < STEP, 0.0, rest) - jnp.dot(
                rest[:, 0:STEP], xt, precision=HI, preferred_element_type=F32
            )
            a_ref[d, 0 : n - STEP, :] = pltpu.roll(new, n - STEP, 1)
            a_ref[d, n - STEP :, :] = pltpu.roll(xt, n - STEP, 1)
        return 0

    lax.fori_loop(start, stop, body, 0)


def arrived(buffer, sem):
    pltpu.make_async_copy(buffer, buffer, sem).wait()


def step_kernel(
    path_devices, scens,
    dates, disc, table_any, states, mask, surrender, terminal, ls_columns, table,
    values_out, coef_out, gram_out, rhs_out,
    pair_a, pair_b, left, right, whole, design, gram, gram_half, gram_acc, gram_in, gram_all,
    rhs_own, rhs_in, rhs0_own, rhs0_in, a_ref, e_ref, r_ref,
    mom, mom_half, mom_acc, x_in, x_sum, seat_out, seat_in, seat_all, full, ls_table, mine, pattern, pick_l, pick_r, y_high, y_low, z_pack,
    low, high, left3, right3, parts, parts_in, mine_part, mine_in,
    gh_s, gh_r, g_s, g_r, ga_s, ga_r, gf_s, gf_r, rhs_s, rhs_r, rhs0_s, rhs0_r,
    half_s, half_r, xr_s, xr_r, sr_s, sr_r, sa_s, sa_r, xa_s, xa_r, fw_s, fw_r, pa_s, pa_r, pb_s, pb_r, own_s,
):
    paths = terminal.shape[1]
    terms = ls_columns.shape[1]
    s, p = lax.axis_index("scen"), lax.axis_index("path")
    core, seat = p % 2, p // 2
    seats = path_devices // 2
    rows = gram_out.shape[0]
    index = s * path_devices + p
    first_own = rows * (index % (128 // rows))
    total_paths = paths * path_devices
    scale = 1.0 / total_paths
    own_scale = 1.0 / (total_paths * scens)
    partner = (s, seat * 2 + 1 - core)

    def path_peer(d):
        return (p + d) % path_devices

    def seat_peer(d):
        return (seat + d) % seats

    def scen_peer(d):
        return (s + d) % scens

    def seat_id(j):
        return (s, j * 2 + core)

    def send(src, dst, send_sem, recv_sem, target):
        return pltpu.make_async_remote_copy(
            src_ref=src, dst_ref=dst, send_sem=send_sem, recv_sem=recv_sem,
            device_id=target, device_id_type=MESH)

    def gram_half_copy():
        return send(gram.at[1 - core], gram_half, gh_s, gh_r, partner)

    def gram_copy(j):
        return send(gram_acc.at[j], gram_in.at[seat], g_s.at[j], g_r.at[seat], seat_id(j))

    def gram_all_copy(j):
        block = gram_all.at[core, seat]
        return send(block, block, ga_s.at[j], ga_r.at[seat], seat_id(j))

    def gram_forward(j):
        block = gram_all.at[core, j]
        return send(block, block, gf_s.at[j], gf_r.at[j], partner)

    def rhs_copy(q):
        return send(rhs_own, rhs_in.at[p], rhs_s.at[q], rhs_r.at[p], (s, q))

    def rhs0_copy(q):
        return send(rhs0_own, rhs0_in.at[p], rhs0_s.at[q], rhs0_r.at[p], (s, q))

    def half_copy():
        return send(mom.at[1 - core], mom_half, half_s, half_r, partner)

    def x_copy(t):
        return send(mom_acc.at[t], x_in.at[s], xr_s.at[t], xr_r.at[s], (t, p))

    def seat_copy(j):
        return send(seat_out.at[j], seat_in.at[seat], sr_s.at[j], sr_r.at[seat], seat_id(j))

    def seat_all_copy(j):
        block = seat_all.at[seat]
        return send(block, block, sa_s.at[j], sa_r.at[seat], seat_id(j))

    def full_copy(t):
        block = full.at[core, s]
        return send(block, block, xa_s.at[t], xa_r.at[s], (t, p))

    def forward_copy(t):
        block = full.at[core, t]
        return send(block, block, fw_s.at[t], fw_r.at[t], partner)

    def part_copy(q):
        return send(parts.at[:, q // 8], parts_in.at[p], pa_s.at[q], pa_r.at[p], (s, q))

    def mine_copy(t):
        return send(mine_part.at[t], mine_in.at[s], pb_s.at[t], pb_r.at[s], (t, p))

    barrier = pltpu.get_barrier_semaphore()

    @pl.loop(1, path_devices)
    def _(d):
        pl.semaphore_signal(barrier, inc=1, device_id=(s, path_peer(d)), device_id_type=MESH)

    @pl.loop(1, scens)
    def _(d):
        pl.semaphore_signal(barrier, inc=1, device_id=(scen_peer(d), p), device_id_type=MESH)

    own_tile = pltpu.make_async_copy(
        table_any.at[:, pl.ds(pl.multiple_of(128 * (index // (128 // rows)), 128), 128)], mine, own_s
    )
    own_tile.start()
    ls_table[...] = ls_columns[...].T

    early = states[dates[0]]
    for backward in (1, 0):
        u = early if backward == 0 else states[dates[1]]
        h = (u * u - 1.0) * ROOT_HALF
        for top in range(0, terms, 32):
            t = ls_table[top : top + 32, :]
            result = None
            for v in range(8):
                degree = jnp.broadcast_to(t[:, v : v + 1], (32, paths))
                level = jnp.where(
                    degree == 1, u[v : v + 1, :], jnp.where(degree == 2, h[v : v + 1, :], 1.0)
                )
                result = level if result is None else result * level
            design[backward, top : top + 32, :] = result.astype(BF16)
        live = design[backward]
        weighted = live * mask[backward : backward + 1, :].astype(F32).astype(BF16)
        g = nt(weighted, live)
        blocks = jnp.concatenate([g[0:128, 0:128], g[128:256, 0:128], g[128:256, 128:256]], axis=0)
        gram[backward] = blocks.reshape(gram.shape[1:])
        if backward == 1:
            rhs_own[...] = add_rows(nt(three_rows(disc[1] * terminal[...]), weighted))

    pl.semaphore_wait(barrier, path_devices - 1 + scens - 1)
    gram_half_copy().start()

    g = early * early - 1.0
    h = g * ROOT_HALF
    one = jnp.ones((1, paths), F32)

    def five(v):
        x, y = early[v : v + 1, :], g[v : v + 1, :]
        return [one, x, y, x * y, y * y]

    for side, first in ((left, 0), (right, 4)):
        side[624:SIDE, :] = jnp.zeros((SIDE - 624, paths), F32)
        products([five(first + v) for v in range(4)], pair_a, pair_b, side, 5)

    gram_half_copy().wait()
    gram_acc[...] = gram[core] + gram_half[...]

    @pl.loop(1, seats)
    def _(d):
        gram_copy(seat_peer(d)).start()

    lh, ll = halves(left[...])
    rh, rl = halves(right[...])
    moments = nt(lh, rh) + nt(lh, rl) + nt(ll, rh)
    for k in range(SIDE // 128):
        low_row = k * SIDE
        while low_row < (k + 1) * SIDE:
            c = low_row // CHUNK
            top_row = min((k + 1) * SIDE, (c + 1) * CHUNK)
            mom[c // scens, c % scens, low_row - c * CHUNK : top_row - c * CHUNK, :] = moments[
                low_row - k * SIDE : top_row - k * SIDE, k * 128 : (k + 1) * 128
            ]
            low_row = top_row
    half_copy().start()

    @pl.loop(1, path_devices)
    def _(d):
        rhs_copy(path_peer(d)).start()

    @pl.loop(1, seats)
    def _(d):
        arrived(gram_in.at[seat_peer(d)], g_r.at[seat_peer(d)])

    def add_gram(d, carry):
        return carry + gram_in[seat_peer(d)]

    gram_all[core, seat] = lax.fori_loop(1, seats, add_gram, gram_acc[seat])

    @pl.loop(1, seats)
    def _(d):
        gram_all_copy(seat_peer(d)).start()

    gram_forward(seat).start()

    half_copy().wait()
    for t in range(scens):
        mom_acc[t] = mom[core, t] + mom_half[t]

    @pl.loop(1, scens)
    def _(d):
        x_copy(scen_peer(d)).start()

    row = lax.broadcasted_iota(jnp.int32, high.shape, 0)
    for first, is_low in ((0, True), (4, False)):
        t = [table[first + v : first + v + 1, :] for v in range(4)]
        code = ((t[0] * 3 + t[1]) * 3 + t[2]) * 3 + t[3]
        hot = jnp.where(row == code, 1.0, 0.0)
        if is_low:
            low[0:PAIRS, :] = hot.astype(BF16)
            low[PAIRS:128, :] = jnp.zeros((128 - PAIRS, hot.shape[1]), BF16)
            low[128 : 128 + PAIRS, :] = hot.astype(BF16)
            low[128 + PAIRS : 256, :] = jnp.zeros((128 - PAIRS, hot.shape[1]), BF16)
        else:
            high[...] = hot

    @pl.loop(1, seats)
    def _(d):
        j = seat_peer(d)
        arrived(gram_all.at[core, j], ga_r.at[j])
        gram_forward(j).start()

    @pl.loop(1, scens)
    def _(d):
        arrived(x_in.at[scen_peer(d)], xr_r.at[scen_peer(d)])

    x_sum[...] = lax.fori_loop(1, scens, lambda d, carry: carry + x_in[scen_peer(d)], mom_acc[s])
    own_part = CHUNK // seats
    for j in range(seats):
        seat_out[j] = x_sum[j * own_part : (j + 1) * own_part, :]

    @pl.loop(1, seats)
    def _(d):
        seat_copy(seat_peer(d)).start()

    @pl.loop(0, seats)
    def _(j):
        arrived(gram_all.at[1 - core, j], gf_r.at[j])

    ri = lax.broadcasted_iota(jnp.int32, (128, 128), 0)
    ci = lax.broadcasted_iota(jnp.int32, (128, 128), 1)
    ridge = jnp.where(ri == ci, 0.05, 0.0)
    for d in range(2):
        stack = gram_all[d].reshape(384, 128) * scale
        corner = stack[128:256, :]
        a_ref[d, 0:128, 0:128] = stack[0:128, :] + ridge
        a_ref[d, 128:256, 0:128] = corner
        a_ref[d, 0:128, 128:256] = corner.T
        a_ref[d, 128:256, 128:256] = stack[256:384, :] + ridge
    steps = terms // STEP
    eliminate(a_ref, e_ref, r_ref, 0, steps // 4)

    @pl.loop(1, seats)
    def _(d):
        arrived(seat_in.at[seat_peer(d)], sr_r.at[seat_peer(d)])

    seat_all[seat] = lax.fori_loop(
        1, seats, lambda d, carry: carry + seat_in[seat_peer(d)], seat_out[seat]
    )

    @pl.loop(1, seats)
    def _(d):
        seat_all_copy(seat_peer(d)).start()

    eliminate(a_ref, e_ref, r_ref, steps // 4, steps // 2)

    @pl.loop(1, seats)
    def _(d):
        arrived(seat_all.at[seat_peer(d)], sa_r.at[seat_peer(d)])

    for j in range(seats):
        full[core, s, j * own_part : (j + 1) * own_part, :] = seat_all[j]

    @pl.loop(1, scens)
    def _(d):
        full_copy(scen_peer(d)).start()

    forward_copy(s).start()
    eliminate(a_ref, e_ref, r_ref, steps // 2, steps)

    @pl.loop(1, path_devices)
    def _(d):
        arrived(rhs_in.at[path_peer(d)], rhs_r.at[path_peer(d)])

    def add_rhs(d, carry):
        return carry + rhs_in[path_peer(d)]

    rhs = lax.fori_loop(1, path_devices, add_rhs, rhs_own[...]) * scale
    coef = -jnp.dot(
        jnp.broadcast_to(rhs, (8, terms)), a_ref[1], precision=HI, preferred_element_type=F32
    )[0:1]
    coef_out[1:2, :] = coef
    continuation = add_rows(nn(three_rows(coef), design[1]))
    payoff = surrender[dates[1]]
    values = disc[1] * terminal[...]
    values = jnp.where(mask[1:2, :] > 0, jnp.maximum(payoff, continuation), values)
    values = disc[0] * values
    weighted = design[0] * mask[0:1, :].astype(F32).astype(BF16)
    rhs0_own[...] = add_rows(nt(three_rows(values), weighted))

    @pl.loop(1, path_devices)
    def _(d):
        rhs0_copy(path_peer(d)).start()

    for out, first in ((left3, 0), (right3, 4)):
        out[80:PAIRS, :] = jnp.zeros((PAIRS - 80, paths), F32)
        levels = [
            [one, early[first + v : first + v + 1, :], h[first + v : first + v + 1, :]]
            for v in range(4)
        ]
        products(levels, pair_a, pair_b, out, 3)
    prow = lax.broadcasted_iota(jnp.int32, (PAIRS, 1), 0)
    plane = lax.broadcasted_iota(jnp.int32, (1, SIDE), 1)
    for v, (three, five_) in enumerate(((27, 125), (9, 25), (3, 5), (1, 1))):
        b = jnp.where(prow < 81, (prow // three) % 3, -9)
        m = jnp.where(plane < 625, (plane // five_) % 5, -20)
        b, m = jnp.broadcast_to(b, (PAIRS, SIDE)), jnp.broadcast_to(m, (PAIRS, SIDE))
        ones = ((b == 0) & (m == 1)) | ((b == 1) & ((m == 0) | (m == 2))) | ((b == 2) & (m == 3))
        pattern[v, 0] = jnp.where(m == b, 1.0, 0.0).astype(BF16)
        pattern[v, 1] = jnp.where(ones, 1.0, 0.0).astype(BF16)
        pattern[v, 2] = jnp.where(m == b + 2, 1.0, 0.0).astype(BF16)

    @pl.loop(1, scens)
    def _(d):
        t = scen_peer(d)
        arrived(full.at[core, t], xa_r.at[t])
        forward_copy(t).start()

    @pl.loop(1, path_devices)
    def _(d):
        arrived(rhs0_in.at[path_peer(d)], rhs0_r.at[path_peer(d)])

    def add_rhs0(d, carry):
        return carry + rhs0_in[path_peer(d)]

    rhs = lax.fori_loop(1, path_devices, add_rhs0, rhs0_own[...]) * scale
    coef = -jnp.dot(
        jnp.broadcast_to(rhs, (8, terms)), a_ref[0], precision=HI, preferred_element_type=F32
    )[0:1]
    coef_out[0:1, :] = coef
    continuation = add_rows(nn(three_rows(coef), design[0]))
    payoff = surrender[dates[0]]
    final = jnp.where(mask[0:1, :] > 0, jnp.maximum(payoff, continuation), values)
    values_out[...] = final

    rounded = final.astype(BF16).astype(F32)
    lh, ll = halves(left3[...] * rounded)
    rh, rl = halves(right3[...])
    wh, wl = halves(nt(rh, lh) + nt(rh, ll) + nt(rl, lh))
    hot = low[0:PAIRS, :]
    picked = jnp.sum((nn(wh, hot) + nn(wl, hot)) * high[...], axis=0, keepdims=True)
    for t in range(parts.shape[0]):
        for q in range(parts.shape[1]):
            k = (t * parts.shape[1] + q) * 128
            parts[t, q] = picked[:, k : k + 128]

    @pl.loop(1, path_devices)
    def _(d):
        part_copy(path_peer(d)).start()

    own_tile.wait()

    @pl.loop(0, rows)
    def _(r):
        def pattern_of(first):
            result = None
            for v in range(4):
                block = pattern[v, mine[first + v, first_own + r]]
                result = block if result is None else result * block
            return result

        pick_l[r] = pattern_of(0)
        pick_r[r] = pattern_of(4)

    @pl.loop(0, scens)
    def _(t):
        arrived(full.at[1 - core, t], fw_r.at[t])

    for k in range(SIDE // 128):
        low_row = k * SIDE
        while low_row < (k + 1) * SIDE:
            c = low_row // CHUNK
            top_row = min((k + 1) * SIDE, (c + 1) * CHUNK)
            whole[low_row - k * SIDE : top_row - k * SIDE, k * 128 : (k + 1) * 128] = full[
                c // scens, c % scens, low_row - c * CHUNK : top_row - c * CHUNK, :
            ]
            low_row = top_row
    mh, ml = halves(whole[...])
    picks = pick_l[...].reshape(rows * PAIRS, SIDE)
    yh, yl = halves(nn(picks, mh) + nn(picks, ml))
    y_high[...] = yh.reshape(y_high.shape)
    y_low[...] = yl.reshape(y_low.shape)

    @pl.loop(1, path_devices)
    def _(d):
        arrived(parts_in.at[path_peer(d)], pa_r.at[path_peer(d)])

    def add_part(d, carry):
        return carry + parts_in[path_peer(d)]

    mine_part[...] = lax.fori_loop(1, path_devices, add_part, parts[:, p // 8])

    @pl.loop(1, scens)
    def _(d):
        mine_copy(scen_peer(d)).start()

    z_pack[...] = jnp.zeros(z_pack.shape, BF16)

    @pl.loop(0, rows)
    def _(r):
        zh, zl = halves(nt(pick_r[r], y_high[r]) + nt(pick_r[r], y_low[r]))
        z_pack[r, :, 0:PAIRS] = zh
        z_pack[r, :, 128 : 128 + PAIRS] = zl

    @pl.loop(1, scens)
    def _(d):
        arrived(mine_in.at[scen_peer(d)], pb_r.at[scen_peer(d)])

    def add_mine(d, carry):
        return carry + mine_in[scen_peer(d)]

    last = lax.fori_loop(1, scens, add_mine, mine_part[s])
    last = pltpu.roll(jnp.broadcast_to(last, (8, 128)), (128 - rows * (p % 8)) % 128, 1)
    rhs_out[...] = last[0:1] * own_scale

    column = None
    for v in range(8):
        factor = jnp.where(table[v : v + 1, :] == 2, ROOT_HALF, 1.0)
        column = factor if column is None else column * factor

    @pl.loop(0, rows // 8)
    def _(block):
        lines = []
        for k in range(8):
            r = block * 8 + k
            own = own_scale
            for v in range(8):
                own = own * jnp.where(mine[v, first_own + r] == 2, ROOT_HALF, 1.0)
            picked = nn(z_pack[r], low[...]) * high[...]
            lines.append(jnp.sum(picked, axis=0, keepdims=True) * (column * own))
        gram_out[pl.ds(pl.multiple_of(block * 8, 8), 8), :] = jnp.concatenate(lines, axis=0)

    gram_forward(seat).wait_send()

    @pl.loop(1, seats)
    def _(d):
        j = seat_peer(d)
        gram_copy(j).wait_send()
        gram_all_copy(j).wait_send()
        gram_forward(j).wait_send()

    @pl.loop(1, path_devices)
    def _(d):
        q = path_peer(d)
        rhs_copy(q).wait_send()
        rhs0_copy(q).wait_send()
        part_copy(q).wait_send()

    @pl.loop(1, seats)
    def _(d):
        j = seat_peer(d)
        seat_copy(j).wait_send()
        seat_all_copy(j).wait_send()

    @pl.loop(1, scens)
    def _(d):
        t = scen_peer(d)
        x_copy(t).wait_send()
        full_copy(t).wait_send()
        mine_copy(t).wait_send()

    @pl.loop(0, scens)
    def _(t):
        forward_copy(t).wait_send()


VMEM = pl.BlockSpec(memory_space=pltpu.VMEM)
SMEM = pl.BlockSpec(memory_space=pltpu.SMEM)
DMA = pltpu.SemaphoreType.DMA


def on_device(
    states, exercise_dates, itm_mask, surrender, terminal, discount, ls_table, proxy_table
):
    scens, path_devices = lax.axis_size("scen"), lax.axis_size("path")
    paths = states.shape[3]
    terms, proxy_terms = ls_table.shape[0], proxy_table.shape[0]
    devices = scens * path_devices
    seats = path_devices // 2
    own_rows = proxy_terms // devices
    columns = proxy_table.T
    rows = 384 // seats
    buffer = pltpu.VMEM
    tiles = proxy_terms // 128

    values, coefficients, proxy_gram, proxy_rhs = pl.pallas_call(
        functools.partial(step_kernel, path_devices, scens),
        out_shape=(
            jax.ShapeDtypeStruct((1, paths), F32),
            jax.ShapeDtypeStruct((2, terms), F32),
            jax.ShapeDtypeStruct((own_rows, proxy_terms), F32),
            jax.ShapeDtypeStruct((1, 128), F32),
        ),
        in_specs=[SMEM] * 2 + [pl.BlockSpec(memory_space=pl.ANY)] + [VMEM] * 6,
        out_specs=[VMEM] * 4,
        scratch_shapes=[
            buffer((32, paths), F32), buffer((32, paths), F32),
            buffer((SIDE, paths), F32), buffer((SIDE, paths), F32),
            buffer((SIDE, SIDE), F32),
            buffer((2, terms, paths), BF16),
            buffer((2, seats, rows, 128), F32),
            buffer((seats, rows, 128), F32), buffer((seats, rows, 128), F32), buffer((seats, rows, 128), F32),
            buffer((2, seats, rows, 128), F32),
            buffer((1, terms), F32), buffer((path_devices, 1, terms), F32),
            buffer((1, terms), F32), buffer((path_devices, 1, terms), F32),
            buffer((2, terms, terms), F32), buffer((8, 8, 128), F32), buffer((8, 128), F32),
            buffer((2, scens, CHUNK, 128), F32),
            buffer((scens, CHUNK, 128), F32), buffer((scens, CHUNK, 128), F32), buffer((scens, CHUNK, 128), F32),
            buffer((CHUNK, 128), F32),
            buffer((seats, CHUNK // seats, 128), F32), buffer((seats, CHUNK // seats, 128), F32),
            buffer((seats, CHUNK // seats, 128), F32),
            buffer((2, scens, CHUNK, 128), F32),
            buffer((terms, 8), jnp.int32),
            pltpu.SMEM((8, 128), jnp.int32),
            buffer((4, 3, PAIRS, SIDE), BF16),
            buffer((own_rows, PAIRS, SIDE), BF16), buffer((own_rows, PAIRS, SIDE), BF16),
            buffer((own_rows, PAIRS, SIDE), BF16), buffer((own_rows, PAIRS, SIDE), BF16),
            buffer((own_rows, PAIRS, 256), BF16),
            buffer((256, proxy_terms), BF16), buffer((PAIRS, proxy_terms), F32),
            buffer((PAIRS, paths), F32), buffer((PAIRS, paths), F32),
            buffer((scens, tiles // scens, 1, 128), F32),
            buffer((path_devices, scens, 1, 128), F32),
            buffer((scens, 1, 128), F32), buffer((scens, 1, 128), F32),
            DMA, DMA,
            DMA((seats,)), DMA((seats,)), DMA((seats,)), DMA((seats,)), DMA((seats,)), DMA((seats,)),
            DMA((path_devices,)), DMA((path_devices,)), DMA((path_devices,)), DMA((path_devices,)),
            DMA, DMA,
            DMA((scens,)), DMA((scens,)), DMA((seats,)), DMA((seats,)), DMA((seats,)), DMA((seats,)),
            DMA((scens,)), DMA((scens,)), DMA((scens,)), DMA((scens,)),
            DMA((path_devices,)), DMA((path_devices,)),
            DMA((scens,)), DMA((scens,)), DMA,
        ],
        compiler_params=pltpu.CompilerParams(collective_id=0, has_side_effects=True),
        name="step",
    )(
        exercise_dates[0], discount[0], columns, states[0], itm_mask[0], surrender.transpose(1, 0, 2), terminal,
        ls_table.T, columns,
    )
    return (values, coefficients[None], proxy_gram, proxy_rhs[0, :own_rows])


def solution(mesh):
    placed = (
        P("scen", None, None, "path"),
        P("scen", None),
        P("scen", None, "path"),
        P("scen", None, "path"),
        P("scen", "path"),
        P("scen", None),
        P(),
        P(),
    )
    return jax.shard_map(
        on_device,
        mesh=mesh,
        in_specs=placed,
        out_specs=(
            P("scen", "path"),
            P("scen", None, None),
            P(("scen", "path"), None),
            P(("scen", "path")),
        ),
        check_vma=False,
    )
```

```python
import functools

import jax
import jax.numpy as jnp
from jax import lax
from jax.experimental import pallas as pl
from jax.experimental.pallas import tpu as pltpu
from jax.sharding import PartitionSpec as P

MESH = pl.DeviceIdType.MESH
HI = lax.Precision.HIGHEST
F32, BF16 = jnp.float32, jnp.bfloat16
ROOT_HALF = 0.7071067811865476
SIDE = 640
CHUNK = 400
PAIRS = 96
STEP = 32


def nt(a, b):
    return lax.dot_general(a, b, (((1,), (1,)), ((), ())), preferred_element_type=F32)


def nn(a, b):
    return jnp.dot(a, b, preferred_element_type=F32)


def halves(x):
    high = x.astype(BF16)
    return high, (x - high.astype(F32)).astype(BF16)


def three_rows(x):
    high = x.astype(BF16).astype(F32)
    rest = x - high
    mid = rest.astype(BF16).astype(F32)
    sub = lax.broadcasted_iota(jnp.int32, (8, x.shape[1]), 0)
    low = rest - mid
    return jnp.where(
        sub == 0, high, jnp.where(sub == 1, mid, jnp.where(sub == 2, low, 0.0))
    ).astype(BF16)


def add_rows(x):
    return x[0:1] + x[1:2] + x[2:3]


def products(factors, pair_a, pair_b, out, levels):
    count = levels * levels
    for i in range(levels):
        for j in range(levels):
            row = i * levels + j
            pair_a[row : row + 1, :] = factors[0][i] * factors[1][j]
            pair_b[row : row + 1, :] = factors[2][i] * factors[3][j]
    for i in range(count):
        out[i * count : (i + 1) * count, :] = pair_a[i : i + 1, :] * pair_b[0:count, :]


def sweep_small(e, n):
    def at(i, j):
        return e[min(i, j), max(i, j)]

    for k in range(0, n, 2):
        p, q, s = e[k, k], e[k, k + 1], e[k + 1, k + 1]
        w = 1.0 / (p * s - q * q)
        pw, qw, sw = p * w, q * w, s * w
        others = [i for i in range(n) if i not in (k, k + 1)]
        r0 = {i: at(k, i) for i in others}
        r1 = {i: at(k + 1, i) for i in others}
        x0 = {i: sw * r0[i] - qw * r1[i] for i in others}
        x1 = {i: pw * r1[i] - qw * r0[i] for i in others}
        for i in others:
            for j in others:
                if i <= j:
                    e[i, j] = e[i, j] - (r0[i] * x0[j] + r1[i] * x1[j])
        for i in others:
            e[min(i, k), max(i, k)] = x0[i]
            e[min(i, k + 1), max(i, k + 1)] = x1[i]
        e[k, k], e[k, k + 1], e[k + 1, k + 1] = -sw, qw, -pw
    return e


def tree_sum(terms):
    while len(terms) > 1:
        terms = [terms[t] + terms[t + 1] for t in range(0, len(terms), 2)]
    return terms[0]


def leaf(a, e_ref, r_ref):
    lane = lax.broadcasted_iota(jnp.int32, (STEP, 128), 1)
    lane8 = lax.broadcasted_iota(jnp.int32, (8, 128), 1)
    sub8 = lax.broadcasted_iota(jnp.int32, (8, 128), 0)
    half = lane - lane % 64
    in_half = lane8 % 64
    for o in range(0, STEP, 8):
        cols = [jnp.take_along_axis(a, half + (o + j), axis=1) for j in range(8)]
        r_ref[...] = a[o : o + 8, :]
        for j in range(8):
            e_ref[j] = cols[j][o : o + 8, :]
        e = {(i, j): e_ref[j, pl.ds(i, 8, stride=0), :] for i in range(8) for j in range(i, 8)}
        e = sweep_small(e, 8)
        rows = [r_ref[pl.ds(i, 8, stride=0), :] for i in range(8)]
        xs = []
        for i in range(8):
            entries = [e[min(i, j), max(i, j)] for j in range(8)]
            x = -tree_sum([entries[j] * rows[j] for j in range(8)])
            for j in range(8):
                x = jnp.where(in_half == o + j, entries[j], x)
            xs.append(x)
        tile = xs[0]
        for i in range(1, 8):
            tile = jnp.where(sub8 == i, xs[i], tile)
        inside = (in_half >= o) & (in_half < o + 8)
        tiles = []
        for t in range(0, STEP, 8):
            if t == o:
                tiles.append(tile)
            else:
                base = jnp.where(inside, 0.0, a[t : t + 8, :])
                tiles.append(base - tree_sum([cols[j][t : t + 8, :] * xs[j] for j in range(8)]))
        a = jnp.concatenate(tiles, axis=0)
    return a


def eliminate(a_ref, e_ref, r_ref, start, stop):
    n = a_ref.shape[1]
    lane = lax.broadcasted_iota(jnp.int32, (STEP, n), 1)
    lane1 = lax.broadcasted_iota(jnp.int32, (STEP, 128), 1)
    lane2 = lax.broadcasted_iota(jnp.int32, (n - STEP, n), 1)

    def body(k, _):
        first = [a_ref[d, 0:STEP, 0:128] for d in range(2)]
        both = leaf(jnp.where(lane1 < 64, first[0], pltpu.roll(first[1], 64, 1)), e_ref, r_ref)
        for d, neg in enumerate((both, pltpu.roll(both, 64, 1))):
            r = a_ref[d, 0:STEP, :]
            rest = a_ref[d, STEP:, :]
            x = jnp.dot(neg[:, 0:STEP], r, precision=HI, preferred_element_type=F32)
            xt = jnp.where(lane < STEP, jnp.concatenate([neg, neg], axis=1), -x)
            new = jnp.where(lane2 < STEP, 0.0, rest) - jnp.dot(
                rest[:, 0:STEP], xt, precision=HI, preferred_element_type=F32
            )
            a_ref[d, 0 : n - STEP, :] = pltpu.roll(new, n - STEP, 1)
            a_ref[d, n - STEP :, :] = pltpu.roll(xt, n - STEP, 1)
        return 0

    lax.fori_loop(start, stop, body, 0)


def arrived(buffer, sem):
    pltpu.make_async_copy(buffer, buffer, sem).wait()


def step_kernel(
    path_devices, scens,
    dates, disc, table_any, states, mask, surrender, terminal, ls_columns, table,
    values_out, coef_out, gram_out, rhs_out,
    pair_a, pair_b, left, right, whole, design, gram, gram_half, gram_acc, gram_in, gram_all,
    rhs_own, rhs_in, rhs0_own, rhs0_in, a_ref, e_ref, r_ref,
    mom, mom_half, mom_acc, x_in, x_sum, seat_out, seat_in, seat_all, full, ls_table, mine, pattern, pick_l, pick_r, y_high, y_low, z_pack,
    low, high, left3, right3, parts, parts_in, mine_part, mine_in,
    gh_s, gh_r, g_s, g_r, ga_s, ga_r, gf_s, gf_r, rhs_s, rhs_r, rhs0_s, rhs0_r,
    half_s, half_r, xr_s, xr_r, sr_s, sr_r, sa_s, sa_r, xa_s, xa_r, fw_s, fw_r, pa_s, pa_r, pb_s, pb_r, own_s,
):
    paths = terminal.shape[1]
    terms = ls_columns.shape[1]
    s, p = lax.axis_index("scen"), lax.axis_index("path")
    core, seat = p % 2, p // 2
    seats = path_devices // 2
    rows = gram_out.shape[0]
    index = s * path_devices + p
    first_own = rows * (index % (128 // rows))
    total_paths = paths * path_devices
    scale = 1.0 / total_paths
    own_scale = 1.0 / (total_paths * scens)
    partner = (s, seat * 2 + 1 - core)

    def path_peer(d):
        return (p + d) % path_devices

    def seat_peer(d):
        return (seat + d) % seats

    def scen_peer(d):
        return (s + d) % scens

    def seat_id(j):
        return (s, j * 2 + core)

    def send(src, dst, send_sem, recv_sem, target):
        return pltpu.make_async_remote_copy(
            src_ref=src, dst_ref=dst, send_sem=send_sem, recv_sem=recv_sem,
            device_id=target, device_id_type=MESH)

    def gram_half_copy():
        return send(gram.at[1 - core], gram_half, gh_s, gh_r, partner)

    def gram_copy(j):
        return send(gram_acc.at[j], gram_in.at[seat], g_s.at[j], g_r.at[seat], seat_id(j))

    def gram_all_copy(j):
        block = gram_all.at[core, seat]
        return send(block, block, ga_s.at[j], ga_r.at[seat], seat_id(j))

    def gram_forward(j):
        block = gram_all.at[core, j]
        return send(block, block, gf_s.at[j], gf_r.at[j], partner)

    def rhs_copy(q):
        return send(rhs_own, rhs_in.at[p], rhs_s.at[q], rhs_r.at[p], (s, q))

    def rhs0_copy(q):
        return send(rhs0_own, rhs0_in.at[p], rhs0_s.at[q], rhs0_r.at[p], (s, q))

    def half_copy(t):
        return send(mom.at[1 - core, t], mom_half.at[t], half_s.at[t], half_r.at[t], partner)

    def x_copy(t):
        return send(mom_acc.at[t], x_in.at[s], xr_s.at[t], xr_r.at[s], (t, p))

    def seat_copy(j):
        return send(seat_out.at[j], seat_in.at[seat], sr_s.at[j], sr_r.at[seat], seat_id(j))

    def seat_all_copy(j):
        block = seat_all.at[seat]
        return send(block, block, sa_s.at[j], sa_r.at[seat], seat_id(j))

    def full_copy(t):
        block = full.at[core, s]
        return send(block, block, xa_s.at[t], xa_r.at[s], (t, p))

    def forward_copy(t):
        block = full.at[core, t]
        return send(block, block, fw_s.at[t], fw_r.at[t], partner)

    def part_copy(q):
        return send(parts.at[:, q // 8], parts_in.at[p], pa_s.at[q], pa_r.at[p], (s, q))

    def mine_copy(t):
        return send(mine_part.at[t], mine_in.at[s], pb_s.at[t], pb_r.at[s], (t, p))

    barrier = pltpu.get_barrier_semaphore()

    @pl.loop(1, path_devices)
    def _(d):
        pl.semaphore_signal(barrier, inc=1, device_id=(s, path_peer(d)), device_id_type=MESH)

    @pl.loop(1, scens)
    def _(d):
        pl.semaphore_signal(barrier, inc=1, device_id=(scen_peer(d), p), device_id_type=MESH)

    own_tile = pltpu.make_async_copy(
        table_any.at[:, pl.ds(pl.multiple_of(128 * (index // (128 // rows)), 128), 128)], mine, own_s
    )
    own_tile.start()
    ls_table[...] = ls_columns[...].T

    early = states[dates[0]]
    for backward in (1, 0):
        u = early if backward == 0 else states[dates[1]]
        h = (u * u - 1.0) * ROOT_HALF
        for top in range(0, terms, 32):
            t = ls_table[top : top + 32, :]
            result = None
            for v in range(8):
                degree = jnp.broadcast_to(t[:, v : v + 1], (32, paths))
                level = jnp.where(
                    degree == 1, u[v : v + 1, :], jnp.where(degree == 2, h[v : v + 1, :], 1.0)
                )
                result = level if result is None else result * level
            design[backward, top : top + 32, :] = result.astype(BF16)
        live = design[backward]
        weighted = live * mask[backward : backward + 1, :].astype(F32).astype(BF16)
        g = nt(weighted, live)
        blocks = jnp.concatenate([g[0:128, 0:128], g[128:256, 0:128], g[128:256, 128:256]], axis=0)
        gram[backward] = blocks.reshape(gram.shape[1:])
        if backward == 1:
            rhs_own[...] = add_rows(nt(three_rows(disc[1] * terminal[...]), weighted))

    pl.semaphore_wait(barrier, path_devices - 1 + scens - 1)
    gram_half_copy().start()

    g = early * early - 1.0
    h = g * ROOT_HALF
    one = jnp.ones((1, paths), F32)

    def five(v):
        x, y = early[v : v + 1, :], g[v : v + 1, :]
        return [one, x, y, x * y, y * y]

    for side, first in ((left, 0), (right, 4)):
        side[624:SIDE, :] = jnp.zeros((SIDE - 624, paths), F32)
        products([five(first + v) for v in range(4)], pair_a, pair_b, side, 5)

    gram_half_copy().wait()
    gram_acc[...] = gram[core] + gram_half[...]

    @pl.loop(1, seats)
    def _(d):
        gram_copy(seat_peer(d)).start()

    lh, ll = halves(left[...])
    rh, rl = halves(right[...])
    moments = nt(lh, rh) + nt(lh, rl) + nt(ll, rh)
    for k in range(SIDE // 128):
        low_row = k * SIDE
        while low_row < (k + 1) * SIDE:
            c = low_row // CHUNK
            top_row = min((k + 1) * SIDE, (c + 1) * CHUNK)
            mom[c // scens, c % scens, low_row - c * CHUNK : top_row - c * CHUNK, :] = moments[
                low_row - k * SIDE : top_row - k * SIDE, k * 128 : (k + 1) * 128
            ]
            low_row = top_row

    @pl.loop(1, scens + 1)
    def _(d):
        half_copy(scen_peer(d)).start()

    @pl.loop(1, path_devices)
    def _(d):
        rhs_copy(path_peer(d)).start()

    @pl.loop(1, seats)
    def _(d):
        arrived(gram_in.at[seat_peer(d)], g_r.at[seat_peer(d)])

    def add_gram(d, carry):
        return carry + gram_in[seat_peer(d)]

    gram_all[core, seat] = lax.fori_loop(1, seats, add_gram, gram_acc[seat])

    @pl.loop(1, seats)
    def _(d):
        gram_all_copy(seat_peer(d)).start()

    gram_forward(seat).start()

    @pl.loop(1, scens)
    def _(d):
        t = scen_peer(d)
        arrived(mom_half.at[t], half_r.at[t])
        mom_acc[t] = mom[core, t] + mom_half[t]
        x_copy(t).start()

    arrived(mom_half.at[s], half_r.at[s])
    mom_acc[s] = mom[core, s] + mom_half[s]

    row = lax.broadcasted_iota(jnp.int32, high.shape, 0)
    for first, is_low in ((0, True), (4, False)):
        t = [table[first + v : first + v + 1, :] for v in range(4)]
        code = ((t[0] * 3 + t[1]) * 3 + t[2]) * 3 + t[3]
        hot = jnp.where(row == code, 1.0, 0.0)
        if is_low:
            low[0:PAIRS, :] = hot.astype(BF16)
            low[PAIRS:128, :] = jnp.zeros((128 - PAIRS, hot.shape[1]), BF16)
            low[128 : 128 + PAIRS, :] = hot.astype(BF16)
            low[128 + PAIRS : 256, :] = jnp.zeros((128 - PAIRS, hot.shape[1]), BF16)
        else:
            high[...] = hot

    @pl.loop(1, seats)
    def _(d):
        j = seat_peer(d)
        arrived(gram_all.at[core, j], ga_r.at[j])
        gram_forward(j).start()

    @pl.loop(0, seats)
    def _(j):
        arrived(gram_all.at[1 - core, j], gf_r.at[j])

    ri = lax.broadcasted_iota(jnp.int32, (128, 128), 0)
    ci = lax.broadcasted_iota(jnp.int32, (128, 128), 1)
    ridge = jnp.where(ri == ci, 0.05, 0.0)
    for d in range(2):
        stack = gram_all[d].reshape(384, 128) * scale
        corner = stack[128:256, :]
        a_ref[d, 0:128, 0:128] = stack[0:128, :] + ridge
        a_ref[d, 128:256, 0:128] = corner
        a_ref[d, 0:128, 128:256] = corner.T
        a_ref[d, 128:256, 128:256] = stack[256:384, :] + ridge
    steps = terms // STEP
    eliminate(a_ref, e_ref, r_ref, 0, steps // 4)

    @pl.loop(1, scens)
    def _(d):
        arrived(x_in.at[scen_peer(d)], xr_r.at[scen_peer(d)])

    x_sum[...] = lax.fori_loop(1, scens, lambda d, carry: carry + x_in[scen_peer(d)], mom_acc[s])
    own_part = CHUNK // seats
    for j in range(seats):
        seat_out[j] = x_sum[j * own_part : (j + 1) * own_part, :]

    @pl.loop(1, seats)
    def _(d):
        seat_copy(seat_peer(d)).start()

    eliminate(a_ref, e_ref, r_ref, steps // 4, steps // 2)

    @pl.loop(1, seats)
    def _(d):
        arrived(seat_in.at[seat_peer(d)], sr_r.at[seat_peer(d)])

    seat_all[seat] = lax.fori_loop(
        1, seats, lambda d, carry: carry + seat_in[seat_peer(d)], seat_out[seat]
    )

    @pl.loop(1, seats)
    def _(d):
        seat_all_copy(seat_peer(d)).start()

    eliminate(a_ref, e_ref, r_ref, steps // 2, 3 * steps // 4)

    @pl.loop(1, seats)
    def _(d):
        arrived(seat_all.at[seat_peer(d)], sa_r.at[seat_peer(d)])

    for j in range(seats):
        full[core, s, j * own_part : (j + 1) * own_part, :] = seat_all[j]

    @pl.loop(1, scens)
    def _(d):
        full_copy(scen_peer(d)).start()

    forward_copy(s).start()
    eliminate(a_ref, e_ref, r_ref, 3 * steps // 4, steps)

    @pl.loop(1, path_devices)
    def _(d):
        arrived(rhs_in.at[path_peer(d)], rhs_r.at[path_peer(d)])

    def add_rhs(d, carry):
        return carry + rhs_in[path_peer(d)]

    rhs = lax.fori_loop(1, path_devices, add_rhs, rhs_own[...]) * scale
    coef = -jnp.dot(
        jnp.broadcast_to(rhs, (8, terms)), a_ref[1], precision=HI, preferred_element_type=F32
    )[0:1]
    coef_out[1:2, :] = coef
    continuation = add_rows(nn(three_rows(coef), design[1]))
    payoff = surrender[dates[1]]
    values = disc[1] * terminal[...]
    values = jnp.where(mask[1:2, :] > 0, jnp.maximum(payoff, continuation), values)
    values = disc[0] * values
    weighted = design[0] * mask[0:1, :].astype(F32).astype(BF16)
    rhs0_own[...] = add_rows(nt(three_rows(values), weighted))

    @pl.loop(1, path_devices)
    def _(d):
        rhs0_copy(path_peer(d)).start()

    for out, first in ((left3, 0), (right3, 4)):
        out[80:PAIRS, :] = jnp.zeros((PAIRS - 80, paths), F32)
        levels = [
            [one, early[first + v : first + v + 1, :], h[first + v : first + v + 1, :]]
            for v in range(4)
        ]
        products(levels, pair_a, pair_b, out, 3)
    prow = lax.broadcasted_iota(jnp.int32, (PAIRS, 1), 0)
    plane = lax.broadcasted_iota(jnp.int32, (1, SIDE), 1)
    for v, (three, five_) in enumerate(((27, 125), (9, 25), (3, 5), (1, 1))):
        b = jnp.where(prow < 81, (prow // three) % 3, -9)
        m = jnp.where(plane < 625, (plane // five_) % 5, -20)
        b, m = jnp.broadcast_to(b, (PAIRS, SIDE)), jnp.broadcast_to(m, (PAIRS, SIDE))
        ones = ((b == 0) & (m == 1)) | ((b == 1) & ((m == 0) | (m == 2))) | ((b == 2) & (m == 3))
        pattern[v, 0] = jnp.where(m == b, 1.0, 0.0).astype(BF16)
        pattern[v, 1] = jnp.where(ones, 1.0, 0.0).astype(BF16)
        pattern[v, 2] = jnp.where(m == b + 2, 1.0, 0.0).astype(BF16)

    own_tile.wait()

    @pl.loop(0, rows)
    def _(r):
        def pattern_of(first):
            result = None
            for v in range(4):
                block = pattern[v, mine[first + v, first_own + r]]
                result = block if result is None else result * block
            return result

        pick_l[r] = pattern_of(0)
        pick_r[r] = pattern_of(4)

    @pl.loop(1, scens)
    def _(d):
        t = scen_peer(d)
        arrived(full.at[core, t], xa_r.at[t])
        forward_copy(t).start()

    @pl.loop(1, path_devices)
    def _(d):
        arrived(rhs0_in.at[path_peer(d)], rhs0_r.at[path_peer(d)])

    def add_rhs0(d, carry):
        return carry + rhs0_in[path_peer(d)]

    rhs = lax.fori_loop(1, path_devices, add_rhs0, rhs0_own[...]) * scale
    coef = -jnp.dot(
        jnp.broadcast_to(rhs, (8, terms)), a_ref[0], precision=HI, preferred_element_type=F32
    )[0:1]
    coef_out[0:1, :] = coef
    continuation = add_rows(nn(three_rows(coef), design[0]))
    payoff = surrender[dates[0]]
    final = jnp.where(mask[0:1, :] > 0, jnp.maximum(payoff, continuation), values)
    values_out[...] = final

    rounded = final.astype(BF16).astype(F32)
    lh, ll = halves(left3[...] * rounded)
    rh, rl = halves(right3[...])
    wh, wl = halves(nt(rh, lh) + nt(rh, ll) + nt(rl, lh))
    hot = low[0:PAIRS, :]
    picked = jnp.sum((nn(wh, hot) + nn(wl, hot)) * high[...], axis=0, keepdims=True)
    for t in range(parts.shape[0]):
        for q in range(parts.shape[1]):
            k = (t * parts.shape[1] + q) * 128
            parts[t, q] = picked[:, k : k + 128]

    @pl.loop(1, path_devices)
    def _(d):
        part_copy(path_peer(d)).start()

    @pl.loop(0, scens)
    def _(t):
        arrived(full.at[1 - core, t], fw_r.at[t])

    for k in range(SIDE // 128):
        low_row = k * SIDE
        while low_row < (k + 1) * SIDE:
            c = low_row // CHUNK
            top_row = min((k + 1) * SIDE, (c + 1) * CHUNK)
            whole[low_row - k * SIDE : top_row - k * SIDE, k * 128 : (k + 1) * 128] = full[
                c // scens, c % scens, low_row - c * CHUNK : top_row - c * CHUNK, :
            ]
            low_row = top_row
    mh, ml = halves(whole[...])
    picks = pick_l[...].reshape(rows * PAIRS, SIDE)
    yh, yl = halves(nn(picks, mh) + nn(picks, ml))
    y_high[...] = yh.reshape(y_high.shape)
    y_low[...] = yl.reshape(y_low.shape)

    def second_product(r):
        zh, zl = halves(nt(pick_r[r], y_high[r]) + nt(pick_r[r], y_low[r]))
        z_pack[r, :, 0:PAIRS] = zh
        z_pack[r, :, 128 : 128 + PAIRS] = zl

    z_pack[...] = jnp.zeros(z_pack.shape, BF16)
    pl.loop(0, rows // 2)(second_product)

    @pl.loop(1, path_devices)
    def _(d):
        arrived(parts_in.at[path_peer(d)], pa_r.at[path_peer(d)])

    def add_part(d, carry):
        return carry + parts_in[path_peer(d)]

    mine_part[...] = lax.fori_loop(1, path_devices, add_part, parts[:, p // 8])

    @pl.loop(1, scens)
    def _(d):
        mine_copy(scen_peer(d)).start()

    pl.loop(rows // 2, rows)(second_product)

    column = None
    for v in range(8):
        factor = jnp.where(table[v : v + 1, :] == 2, ROOT_HALF, 1.0)
        column = factor if column is None else column * factor

    @pl.loop(0, rows // 8)
    def _(block):
        lines = []
        for k in range(8):
            r = block * 8 + k
            own = own_scale
            for v in range(8):
                own = own * jnp.where(mine[v, first_own + r] == 2, ROOT_HALF, 1.0)
            picked = nn(z_pack[r], low[...]) * high[...]
            lines.append(jnp.sum(picked, axis=0, keepdims=True) * (column * own))
        gram_out[pl.ds(pl.multiple_of(block * 8, 8), 8), :] = jnp.concatenate(lines, axis=0)

    @pl.loop(1, scens)
    def _(d):
        arrived(mine_in.at[scen_peer(d)], pb_r.at[scen_peer(d)])

    def add_mine(d, carry):
        return carry + mine_in[scen_peer(d)]

    last = lax.fori_loop(1, scens, add_mine, mine_part[s])
    last = pltpu.roll(jnp.broadcast_to(last, (8, 128)), (128 - rows * (p % 8)) % 128, 1)
    rhs_out[...] = last[0:1] * own_scale

    gram_forward(seat).wait_send()

    @pl.loop(1, seats)
    def _(d):
        j = seat_peer(d)
        gram_copy(j).wait_send()
        gram_all_copy(j).wait_send()
        gram_forward(j).wait_send()

    @pl.loop(1, path_devices)
    def _(d):
        q = path_peer(d)
        rhs_copy(q).wait_send()
        rhs0_copy(q).wait_send()
        part_copy(q).wait_send()

    @pl.loop(1, seats)
    def _(d):
        j = seat_peer(d)
        seat_copy(j).wait_send()
        seat_all_copy(j).wait_send()

    @pl.loop(1, scens)
    def _(d):
        t = scen_peer(d)
        x_copy(t).wait_send()
        full_copy(t).wait_send()
        mine_copy(t).wait_send()

    @pl.loop(0, scens)
    def _(t):
        half_copy(t).wait_send()
        forward_copy(t).wait_send()


def finish_kernel(values, coef, gram, rhs, values_out, coef_out, gram_out, rhs_out):
    values_out[...] = values[...]
    coef_out[...] = coef[...]
    gram_out[...] = gram[...]
    rhs_out[...] = rhs[:, 0 : rhs_out.shape[1]]


VMEM = pl.BlockSpec(memory_space=pltpu.VMEM)
SMEM = pl.BlockSpec(memory_space=pltpu.SMEM)
DMA = pltpu.SemaphoreType.DMA


def on_device(
    states, exercise_dates, itm_mask, surrender, terminal, discount, ls_table, proxy_table
):
    scens, path_devices = lax.axis_size("scen"), lax.axis_size("path")
    paths = states.shape[3]
    terms, proxy_terms = ls_table.shape[0], proxy_table.shape[0]
    devices = scens * path_devices
    seats = path_devices // 2
    own_rows = proxy_terms // devices
    columns = proxy_table.T
    rows = 384 // seats
    buffer = pltpu.VMEM
    tiles = proxy_terms // 128

    values, coefficients, proxy_gram, proxy_rhs = pl.pallas_call(
        functools.partial(step_kernel, path_devices, scens),
        out_shape=(
            jax.ShapeDtypeStruct((1, paths), F32),
            jax.ShapeDtypeStruct((2, terms), F32),
            jax.ShapeDtypeStruct((own_rows, proxy_terms), F32),
            jax.ShapeDtypeStruct((1, 128), F32),
        ),
        in_specs=[SMEM] * 2 + [pl.BlockSpec(memory_space=pl.ANY)] + [VMEM] * 6,
        out_specs=[VMEM] * 4,
        scratch_shapes=[
            buffer((32, paths), F32), buffer((32, paths), F32),
            buffer((SIDE, paths), F32), buffer((SIDE, paths), F32),
            buffer((SIDE, SIDE), F32),
            buffer((2, terms, paths), BF16),
            buffer((2, seats, rows, 128), F32),
            buffer((seats, rows, 128), F32), buffer((seats, rows, 128), F32), buffer((seats, rows, 128), F32),
            buffer((2, seats, rows, 128), F32),
            buffer((1, terms), F32), buffer((path_devices, 1, terms), F32),
            buffer((1, terms), F32), buffer((path_devices, 1, terms), F32),
            buffer((2, terms, terms), F32), buffer((8, 8, 128), F32), buffer((8, 128), F32),
            buffer((2, scens, CHUNK, 128), F32),
            buffer((scens, CHUNK, 128), F32), buffer((scens, CHUNK, 128), F32), buffer((scens, CHUNK, 128), F32),
            buffer((CHUNK, 128), F32),
            buffer((seats, CHUNK // seats, 128), F32), buffer((seats, CHUNK // seats, 128), F32),
            buffer((seats, CHUNK // seats, 128), F32),
            buffer((2, scens, CHUNK, 128), F32),
            buffer((terms, 8), jnp.int32),
            pltpu.SMEM((8, 128), jnp.int32),
            buffer((4, 3, PAIRS, SIDE), BF16),
            buffer((own_rows, PAIRS, SIDE), BF16), buffer((own_rows, PAIRS, SIDE), BF16),
            buffer((own_rows, PAIRS, SIDE), BF16), buffer((own_rows, PAIRS, SIDE), BF16),
            buffer((own_rows, PAIRS, 256), BF16),
            buffer((256, proxy_terms), BF16), buffer((PAIRS, proxy_terms), F32),
            buffer((PAIRS, paths), F32), buffer((PAIRS, paths), F32),
            buffer((scens, tiles // scens, 1, 128), F32),
            buffer((path_devices, scens, 1, 128), F32),
            buffer((scens, 1, 128), F32), buffer((scens, 1, 128), F32),
            DMA, DMA,
            DMA((seats,)), DMA((seats,)), DMA((seats,)), DMA((seats,)), DMA((seats,)), DMA((seats,)),
            DMA((path_devices,)), DMA((path_devices,)), DMA((path_devices,)), DMA((path_devices,)),
            DMA((scens,)), DMA((scens,)),
            DMA((scens,)), DMA((scens,)), DMA((seats,)), DMA((seats,)), DMA((seats,)), DMA((seats,)),
            DMA((scens,)), DMA((scens,)), DMA((scens,)), DMA((scens,)),
            DMA((path_devices,)), DMA((path_devices,)),
            DMA((scens,)), DMA((scens,)), DMA,
        ],
        compiler_params=pltpu.CompilerParams(collective_id=0, has_side_effects=True),
        name="step",
    )(
        exercise_dates[0], discount[0], columns, states[0], itm_mask[0], surrender.transpose(1, 0, 2), terminal,
        ls_table.T, columns,
    )
    values, coefficients, proxy_gram, proxy_rhs = pl.pallas_call(
        finish_kernel,
        out_shape=(
            jax.ShapeDtypeStruct((1, paths), F32),
            jax.ShapeDtypeStruct((2, terms), F32),
            jax.ShapeDtypeStruct((own_rows, proxy_terms), F32),
            jax.ShapeDtypeStruct((1, own_rows), F32),
        ),
        in_specs=[VMEM] * 4,
        out_specs=[VMEM] * 4,
        name="finish",
    )(values, coefficients, proxy_gram, proxy_rhs)
    return (values, coefficients[None], proxy_gram, proxy_rhs[0])


def solution(mesh):
    placed = (
        P("scen", None, None, "path"),
        P("scen", None),
        P("scen", None, "path"),
        P("scen", None, "path"),
        P("scen", "path"),
        P("scen", None),
        P(),
        P(),
    )
    return jax.shard_map(
        on_device,
        mesh=mesh,
        in_specs=placed,
        out_specs=(
            P("scen", "path"),
            P("scen", None, None),
            P(("scen", "path"), None),
            P(("scen", "path")),
        ),
        check_vma=False,
    )
```

```python
import functools

import jax
import jax.numpy as jnp
from jax import lax
from jax.experimental import pallas as pl
from jax.experimental.pallas import tpu as pltpu
from jax.sharding import PartitionSpec as P

MESH = pl.DeviceIdType.MESH
HI = lax.Precision.HIGHEST
F32, BF16 = jnp.float32, jnp.bfloat16
ROOT_HALF = 0.7071067811865476
SIDE = 640
CHUNK = 400
PAIRS = 96
STEP = 32


def nt(a, b):
    return lax.dot_general(a, b, (((1,), (1,)), ((), ())), preferred_element_type=F32)


def nn(a, b):
    return jnp.dot(a, b, preferred_element_type=F32)


def halves(x):
    high = x.astype(BF16)
    return high, (x - high.astype(F32)).astype(BF16)


def three_rows(x):
    high = x.astype(BF16).astype(F32)
    rest = x - high
    mid = rest.astype(BF16).astype(F32)
    sub = lax.broadcasted_iota(jnp.int32, (8, x.shape[1]), 0)
    low = rest - mid
    return jnp.where(
        sub == 0, high, jnp.where(sub == 1, mid, jnp.where(sub == 2, low, 0.0))
    ).astype(BF16)


def add_rows(x):
    return x[0:1] + x[1:2] + x[2:3]


def products(factors, pair_a, pair_b, out, levels):
    count = levels * levels
    for i in range(levels):
        for j in range(levels):
            row = i * levels + j
            pair_a[row : row + 1, :] = factors[0][i] * factors[1][j]
            pair_b[row : row + 1, :] = factors[2][i] * factors[3][j]
    for i in range(count):
        out[i * count : (i + 1) * count, :] = pair_a[i : i + 1, :] * pair_b[0:count, :]


def sweep_small(e, n):
    def at(i, j):
        return e[min(i, j), max(i, j)]

    for k in range(0, n, 2):
        p, q, s = e[k, k], e[k, k + 1], e[k + 1, k + 1]
        w = 1.0 / (p * s - q * q)
        pw, qw, sw = p * w, q * w, s * w
        others = [i for i in range(n) if i not in (k, k + 1)]
        r0 = {i: at(k, i) for i in others}
        r1 = {i: at(k + 1, i) for i in others}
        x0 = {i: sw * r0[i] - qw * r1[i] for i in others}
        x1 = {i: pw * r1[i] - qw * r0[i] for i in others}
        for i in others:
            for j in others:
                if i <= j:
                    e[i, j] = e[i, j] - (r0[i] * x0[j] + r1[i] * x1[j])
        for i in others:
            e[min(i, k), max(i, k)] = x0[i]
            e[min(i, k + 1), max(i, k + 1)] = x1[i]
        e[k, k], e[k, k + 1], e[k + 1, k + 1] = -sw, qw, -pw
    return e


def tree_sum(terms):
    while len(terms) > 1:
        terms = [terms[t] + terms[t + 1] for t in range(0, len(terms), 2)]
    return terms[0]


def leaf(a, e_ref, r_ref):
    lane = lax.broadcasted_iota(jnp.int32, (STEP, 128), 1)
    lane8 = lax.broadcasted_iota(jnp.int32, (8, 128), 1)
    sub8 = lax.broadcasted_iota(jnp.int32, (8, 128), 0)
    half = lane - lane % 64
    in_half = lane8 % 64
    for o in range(0, STEP, 8):
        cols = [jnp.take_along_axis(a, half + (o + j), axis=1) for j in range(8)]
        r_ref[...] = a[o : o + 8, :]
        for j in range(8):
            e_ref[j] = cols[j][o : o + 8, :]
        e = {(i, j): e_ref[j, pl.ds(i, 8, stride=0), :] for i in range(8) for j in range(i, 8)}
        e = sweep_small(e, 8)
        rows = [r_ref[pl.ds(i, 8, stride=0), :] for i in range(8)]
        xs = []
        for i in range(8):
            entries = [e[min(i, j), max(i, j)] for j in range(8)]
            x = -tree_sum([entries[j] * rows[j] for j in range(8)])
            for j in range(8):
                x = jnp.where(in_half == o + j, entries[j], x)
            xs.append(x)
        tile = xs[0]
        for i in range(1, 8):
            tile = jnp.where(sub8 == i, xs[i], tile)
        inside = (in_half >= o) & (in_half < o + 8)
        tiles = []
        for t in range(0, STEP, 8):
            if t == o:
                tiles.append(tile)
            else:
                base = jnp.where(inside, 0.0, a[t : t + 8, :])
                tiles.append(base - tree_sum([cols[j][t : t + 8, :] * xs[j] for j in range(8)]))
        a = jnp.concatenate(tiles, axis=0)
    return a


def eliminate(a_ref, e_ref, r_ref, start, stop):
    n = a_ref.shape[1]
    lane = lax.broadcasted_iota(jnp.int32, (STEP, n), 1)
    lane1 = lax.broadcasted_iota(jnp.int32, (STEP, 128), 1)
    lane2 = lax.broadcasted_iota(jnp.int32, (n - STEP, n), 1)

    def body(k, _):
        first = [a_ref[d, 0:STEP, 0:128] for d in range(2)]
        both = leaf(jnp.where(lane1 < 64, first[0], pltpu.roll(first[1], 64, 1)), e_ref, r_ref)
        for d, neg in enumerate((both, pltpu.roll(both, 64, 1))):
            r = a_ref[d, 0:STEP, :]
            rest = a_ref[d, STEP:, :]
            x = jnp.dot(neg[:, 0:STEP], r, precision=HI, preferred_element_type=F32)
            xt = jnp.where(lane < STEP, jnp.concatenate([neg, neg], axis=1), -x)
            new = jnp.where(lane2 < STEP, 0.0, rest) - jnp.dot(
                rest[:, 0:STEP], xt, precision=HI, preferred_element_type=F32
            )
            a_ref[d, 0 : n - STEP, :] = pltpu.roll(new, n - STEP, 1)
            a_ref[d, n - STEP :, :] = pltpu.roll(xt, n - STEP, 1)
        return 0

    lax.fori_loop(start, stop, body, 0)


def arrived(buffer, sem):
    pltpu.make_async_copy(buffer, buffer, sem).wait()


def step_kernel(
    path_devices, scens,
    dates, disc, table_any, states, mask, surrender, terminal, ls_columns, table,
    values_out, coef_out, gram_out, rhs_out,
    pair_a, pair_b, left, right, whole, design, gram, gram_half, gram_acc, gram_in, gram_all,
    rhs_own, rhs_in, rhs0_own, rhs0_in, a_ref, e_ref, r_ref,
    mom, mom_half, mom_acc, x_in, x_sum, seat_out, seat_in, seat_all, full, ls_table, mine, pattern, pick_l, pick_r, y_high, y_low, z_pack,
    low, high, left3, right3, parts, parts_in, mine_part, mine_in,
    gh_s, gh_r, g_s, g_r, ga_s, ga_r, gf_s, gf_r, rhs_s, rhs_r, rhs0_s, rhs0_r,
    half_s, half_r, xr_s, xr_r, sr_s, sr_r, sa_s, sa_r, xa_s, xa_r, fw_s, fw_r, pa_s, pa_r, pb_s, pb_r, own_s,
):
    paths = terminal.shape[1]
    terms = ls_columns.shape[1]
    s, p = lax.axis_index("scen"), lax.axis_index("path")
    core, seat = p % 2, p // 2
    seats = path_devices // 2
    rows = gram_out.shape[0]
    index = s * path_devices + p
    first_own = rows * (index % (128 // rows))
    total_paths = paths * path_devices
    scale = 1.0 / total_paths
    own_scale = 1.0 / (total_paths * scens)
    partner = (s, seat * 2 + 1 - core)

    def path_peer(d):
        return (p + d) % path_devices

    def seat_peer(d):
        return (seat + d) % seats

    def scen_peer(d):
        return (s + d) % scens

    def seat_id(j):
        return (s, j * 2 + core)

    def send(src, dst, send_sem, recv_sem, target):
        return pltpu.make_async_remote_copy(
            src_ref=src, dst_ref=dst, send_sem=send_sem, recv_sem=recv_sem,
            device_id=target, device_id_type=MESH)

    def gram_half_copy():
        return send(gram.at[1 - core], gram_half, gh_s, gh_r, partner)

    def gram_copy(j):
        return send(gram_acc.at[j], gram_in.at[seat], g_s, g_r, seat_id(j))

    def gram_all_copy(j):
        block = gram_all.at[core, seat]
        return send(block, block, ga_s, ga_r, seat_id(j))

    def gram_forward():
        return send(gram_all.at[core], gram_all.at[core], gf_s, gf_r, partner)

    def rhs_copy(q):
        return send(rhs_own, rhs_in.at[p], rhs_s, rhs_r, (s, q))

    def rhs0_copy(q):
        return send(rhs0_own, rhs0_in.at[p], rhs0_s, rhs0_r, (s, q))

    def half_copy(t):
        return send(mom.at[1 - core, t], mom_half.at[t], half_s.at[t], half_r.at[t], partner)

    def x_copy(t):
        return send(mom_acc.at[t], x_in.at[s], xr_s.at[t], xr_r.at[s], (t, p))

    def seat_copy(j):
        return send(seat_out.at[j], seat_in.at[seat], sr_s.at[j], sr_r.at[seat], seat_id(j))

    def seat_all_copy(j):
        block = seat_all.at[seat]
        return send(block, block, sa_s.at[j], sa_r.at[seat], seat_id(j))

    def full_copy(t):
        block = full.at[core, s]
        return send(block, block, xa_s.at[t], xa_r.at[s], (t, p))

    def forward_copy(t):
        block = full.at[core, t]
        return send(block, block, fw_s.at[t], fw_r.at[t], partner)

    def part_copy(q):
        return send(parts.at[:, q // 8], parts_in.at[p], pa_s, pa_r, (s, q))

    def mine_copy(t):
        return send(mine_part.at[t], mine_in.at[s], pb_s.at[t], pb_r.at[s], (t, p))

    barrier = pltpu.get_barrier_semaphore()

    @pl.loop(1, path_devices)
    def _(d):
        pl.semaphore_signal(barrier, inc=1, device_id=(s, path_peer(d)), device_id_type=MESH)

    @pl.loop(1, scens)
    def _(d):
        pl.semaphore_signal(barrier, inc=1, device_id=(scen_peer(d), p), device_id_type=MESH)

    own_tile = pltpu.make_async_copy(
        table_any.at[:, pl.ds(pl.multiple_of(128 * (index // (128 // rows)), 128), 128)], mine, own_s
    )
    own_tile.start()
    ls_table[...] = ls_columns[...].T

    early = states[dates[0]]
    for backward in (1, 0):
        u = early if backward == 0 else states[dates[1]]
        h = (u * u - 1.0) * ROOT_HALF
        for top in range(0, terms, 32):
            t = ls_table[top : top + 32, :]
            result = None
            for v in range(8):
                degree = jnp.broadcast_to(t[:, v : v + 1], (32, paths))
                level = jnp.where(
                    degree == 1, u[v : v + 1, :], jnp.where(degree == 2, h[v : v + 1, :], 1.0)
                )
                result = level if result is None else result * level
            design[backward, top : top + 32, :] = result.astype(BF16)
        live = design[backward]
        weighted = live * mask[backward : backward + 1, :].astype(F32).astype(BF16)
        g = nt(weighted, live)
        blocks = jnp.concatenate([g[0:128, 0:128], g[128:256, 0:128], g[128:256, 128:256]], axis=0)
        gram[backward] = blocks.reshape(gram.shape[1:])
        if backward == 1:
            rhs_own[...] = add_rows(nt(three_rows(disc[1] * terminal[...]), weighted))

    pl.semaphore_wait(barrier, path_devices - 1 + scens - 1)
    gram_half_copy().start()

    g = early * early - 1.0
    h = g * ROOT_HALF
    one = jnp.ones((1, paths), F32)

    def five(v):
        x, y = early[v : v + 1, :], g[v : v + 1, :]
        return [one, x, y, x * y, y * y]

    for side, first in ((left, 0), (right, 4)):
        side[624:SIDE, :] = jnp.zeros((SIDE - 624, paths), F32)
        products([five(first + v) for v in range(4)], pair_a, pair_b, side, 5)

    gram_half_copy().wait()
    gram_acc[...] = gram[core] + gram_half[...]

    @pl.loop(1, seats)
    def _(d):
        gram_copy(seat_peer(d)).start()

    lh, ll = halves(left[...])
    rh, rl = halves(right[...])
    moments = nt(lh, rh) + nt(lh, rl) + nt(ll, rh)
    for k in range(SIDE // 128):
        low_row = k * SIDE
        while low_row < (k + 1) * SIDE:
            c = low_row // CHUNK
            top_row = min((k + 1) * SIDE, (c + 1) * CHUNK)
            mom[c // scens, c % scens, low_row - c * CHUNK : top_row - c * CHUNK, :] = moments[
                low_row - k * SIDE : top_row - k * SIDE, k * 128 : (k + 1) * 128
            ]
            low_row = top_row

    @pl.loop(1, scens + 1)
    def _(d):
        half_copy(scen_peer(d)).start()

    @pl.loop(1, path_devices)
    def _(d):
        rhs_copy(path_peer(d)).start()

    arrived(gram_in.at[pl.ds(0, seats - 1)], g_r)

    def add_gram(d, carry):
        return carry + gram_in[seat_peer(d)]

    gram_all[core, seat] = lax.fori_loop(1, seats, add_gram, gram_acc[seat])

    @pl.loop(1, seats)
    def _(d):
        gram_all_copy(seat_peer(d)).start()


    @pl.loop(1, scens)
    def _(d):
        t = scen_peer(d)
        arrived(mom_half.at[t], half_r.at[t])
        mom_acc[t] = mom[core, t] + mom_half[t]
        x_copy(t).start()

    arrived(mom_half.at[s], half_r.at[s])
    mom_acc[s] = mom[core, s] + mom_half[s]

    row = lax.broadcasted_iota(jnp.int32, high.shape, 0)
    for first, is_low in ((0, True), (4, False)):
        t = [table[first + v : first + v + 1, :] for v in range(4)]
        code = ((t[0] * 3 + t[1]) * 3 + t[2]) * 3 + t[3]
        hot = jnp.where(row == code, 1.0, 0.0)
        if is_low:
            low[0:PAIRS, :] = hot.astype(BF16)
            low[PAIRS:128, :] = jnp.zeros((128 - PAIRS, hot.shape[1]), BF16)
            low[128 : 128 + PAIRS, :] = hot.astype(BF16)
            low[128 + PAIRS : 256, :] = jnp.zeros((128 - PAIRS, hot.shape[1]), BF16)
        else:
            high[...] = hot

    arrived(gram_all.at[core, pl.ds(0, seats - 1)], ga_r)
    gram_forward().start()

    arrived(gram_all.at[1 - core], gf_r)

    ri = lax.broadcasted_iota(jnp.int32, (128, 128), 0)
    ci = lax.broadcasted_iota(jnp.int32, (128, 128), 1)
    ridge = jnp.where(ri == ci, 0.05, 0.0)
    for d in range(2):
        stack = gram_all[d].reshape(384, 128) * scale
        corner = stack[128:256, :]
        a_ref[d, 0:128, 0:128] = stack[0:128, :] + ridge
        a_ref[d, 128:256, 0:128] = corner
        a_ref[d, 0:128, 128:256] = corner.T
        a_ref[d, 128:256, 128:256] = stack[256:384, :] + ridge
    steps = terms // STEP
    eliminate(a_ref, e_ref, r_ref, 0, steps // 4)

    @pl.loop(1, scens)
    def _(d):
        arrived(x_in.at[scen_peer(d)], xr_r.at[scen_peer(d)])

    x_sum[...] = lax.fori_loop(1, scens, lambda d, carry: carry + x_in[scen_peer(d)], mom_acc[s])
    own_part = CHUNK // seats
    for j in range(seats):
        seat_out[j] = x_sum[j * own_part : (j + 1) * own_part, :]

    @pl.loop(1, seats)
    def _(d):
        seat_copy(seat_peer(d)).start()

    eliminate(a_ref, e_ref, r_ref, steps // 4, steps // 2)

    @pl.loop(1, seats)
    def _(d):
        arrived(seat_in.at[seat_peer(d)], sr_r.at[seat_peer(d)])

    seat_all[seat] = lax.fori_loop(
        1, seats, lambda d, carry: carry + seat_in[seat_peer(d)], seat_out[seat]
    )

    @pl.loop(1, seats)
    def _(d):
        seat_all_copy(seat_peer(d)).start()

    eliminate(a_ref, e_ref, r_ref, steps // 2, 3 * steps // 4)

    @pl.loop(1, seats)
    def _(d):
        arrived(seat_all.at[seat_peer(d)], sa_r.at[seat_peer(d)])

    for j in range(seats):
        full[core, s, j * own_part : (j + 1) * own_part, :] = seat_all[j]

    @pl.loop(1, scens)
    def _(d):
        full_copy(scen_peer(d)).start()

    forward_copy(s).start()
    eliminate(a_ref, e_ref, r_ref, 3 * steps // 4, steps)

    arrived(rhs_in.at[pl.ds(0, path_devices - 1)], rhs_r)

    def add_rhs(d, carry):
        return carry + rhs_in[path_peer(d)]

    rhs = lax.fori_loop(1, path_devices, add_rhs, rhs_own[...]) * scale
    coef = -jnp.dot(
        jnp.broadcast_to(rhs, (8, terms)), a_ref[1], precision=HI, preferred_element_type=F32
    )[0:1]
    coef_out[1:2, :] = coef
    continuation = add_rows(nn(three_rows(coef), design[1]))
    payoff = surrender[dates[1]]
    values = disc[1] * terminal[...]
    values = jnp.where(mask[1:2, :] > 0, jnp.maximum(payoff, continuation), values)
    values = disc[0] * values
    weighted = design[0] * mask[0:1, :].astype(F32).astype(BF16)
    rhs0_own[...] = add_rows(nt(three_rows(values), weighted))

    @pl.loop(1, path_devices)
    def _(d):
        rhs0_copy(path_peer(d)).start()

    for out, first in ((left3, 0), (right3, 4)):
        out[80:PAIRS, :] = jnp.zeros((PAIRS - 80, paths), F32)
        levels = [
            [one, early[first + v : first + v + 1, :], h[first + v : first + v + 1, :]]
            for v in range(4)
        ]
        products(levels, pair_a, pair_b, out, 3)
    prow = lax.broadcasted_iota(jnp.int32, (PAIRS, 1), 0)
    plane = lax.broadcasted_iota(jnp.int32, (1, SIDE), 1)
    for v, (three, five_) in enumerate(((27, 125), (9, 25), (3, 5), (1, 1))):
        b = jnp.where(prow < 81, (prow // three) % 3, -9)
        m = jnp.where(plane < 625, (plane // five_) % 5, -20)
        b, m = jnp.broadcast_to(b, (PAIRS, SIDE)), jnp.broadcast_to(m, (PAIRS, SIDE))
        ones = ((b == 0) & (m == 1)) | ((b == 1) & ((m == 0) | (m == 2))) | ((b == 2) & (m == 3))
        pattern[v, 0] = jnp.where(m == b, 1.0, 0.0).astype(BF16)
        pattern[v, 1] = jnp.where(ones, 1.0, 0.0).astype(BF16)
        pattern[v, 2] = jnp.where(m == b + 2, 1.0, 0.0).astype(BF16)

    own_tile.wait()

    @pl.loop(0, rows)
    def _(r):
        def pattern_of(first):
            result = None
            for v in range(4):
                block = pattern[v, mine[first + v, first_own + r]]
                result = block if result is None else result * block
            return result

        pick_l[r] = pattern_of(0)
        pick_r[r] = pattern_of(4)

    arrived(gram_in.at[pl.ds(0, seats - 1)], g_s)
    arrived(gram_in.at[pl.ds(0, seats - 1)], ga_s)
    arrived(gram_all.at[core], gf_s)
    arrived(rhs_in.at[pl.ds(0, path_devices - 1)], rhs_s)

    @pl.loop(1, seats)
    def _(d):
        j = seat_peer(d)
        seat_copy(j).wait_send()
        seat_all_copy(j).wait_send()

    @pl.loop(1, scens)
    def _(d):
        x_copy(scen_peer(d)).wait_send()

    @pl.loop(0, scens)
    def _(t):
        half_copy(t).wait_send()

    @pl.loop(1, scens)
    def _(d):
        t = scen_peer(d)
        arrived(full.at[core, t], xa_r.at[t])
        forward_copy(t).start()

    arrived(rhs0_in.at[pl.ds(0, path_devices - 1)], rhs0_r)
    arrived(rhs0_in.at[pl.ds(0, path_devices - 1)], rhs0_s)

    def add_rhs0(d, carry):
        return carry + rhs0_in[path_peer(d)]

    rhs = lax.fori_loop(1, path_devices, add_rhs0, rhs0_own[...]) * scale
    coef = -jnp.dot(
        jnp.broadcast_to(rhs, (8, terms)), a_ref[0], precision=HI, preferred_element_type=F32
    )[0:1]
    coef_out[0:1, :] = coef
    continuation = add_rows(nn(three_rows(coef), design[0]))
    payoff = surrender[dates[0]]
    final = jnp.where(mask[0:1, :] > 0, jnp.maximum(payoff, continuation), values)
    values_out[...] = final

    rounded = final.astype(BF16).astype(F32)
    lh, ll = halves(left3[...] * rounded)
    rh, rl = halves(right3[...])
    wh, wl = halves(nt(rh, lh) + nt(rh, ll) + nt(rl, lh))
    hot = low[0:PAIRS, :]
    picked = jnp.sum((nn(wh, hot) + nn(wl, hot)) * high[...], axis=0, keepdims=True)
    for t in range(parts.shape[0]):
        for q in range(parts.shape[1]):
            k = (t * parts.shape[1] + q) * 128
            parts[t, q] = picked[:, k : k + 128]

    @pl.loop(1, path_devices)
    def _(d):
        part_copy(path_peer(d)).start()

    @pl.loop(0, scens)
    def _(t):
        arrived(full.at[1 - core, t], fw_r.at[t])

    for k in range(SIDE // 128):
        low_row = k * SIDE
        while low_row < (k + 1) * SIDE:
            c = low_row // CHUNK
            top_row = min((k + 1) * SIDE, (c + 1) * CHUNK)
            whole[low_row - k * SIDE : top_row - k * SIDE, k * 128 : (k + 1) * 128] = full[
                c // scens, c % scens, low_row - c * CHUNK : top_row - c * CHUNK, :
            ]
            low_row = top_row
    mh, ml = halves(whole[...])
    picks = pick_l[...].reshape(rows * PAIRS, SIDE)
    yh, yl = halves(nn(picks, mh) + nn(picks, ml))
    y_high[...] = yh.reshape(y_high.shape)
    y_low[...] = yl.reshape(y_low.shape)

    def second_product(r):
        zh, zl = halves(nt(pick_r[r], y_high[r]) + nt(pick_r[r], y_low[r]))
        z_pack[r, :, 0:PAIRS] = zh
        z_pack[r, :, 128 : 128 + PAIRS] = zl

    z_pack[...] = jnp.zeros(z_pack.shape, BF16)
    pl.loop(0, rows // 2)(second_product)

    arrived(parts_in.at[pl.ds(0, path_devices - 1)], pa_r)

    def add_part(d, carry):
        return carry + parts_in[path_peer(d)]

    mine_part[...] = lax.fori_loop(1, path_devices, add_part, parts[:, p // 8])

    @pl.loop(1, scens)
    def _(d):
        mine_copy(scen_peer(d)).start()

    pl.loop(rows // 2, rows)(second_product)

    column = None
    for v in range(8):
        factor = jnp.where(table[v : v + 1, :] == 2, ROOT_HALF, 1.0)
        column = factor if column is None else column * factor

    @pl.loop(0, rows // 8)
    def _(block):
        lines = []
        for k in range(8):
            r = block * 8 + k
            own = own_scale
            for v in range(8):
                own = own * jnp.where(mine[v, first_own + r] == 2, ROOT_HALF, 1.0)
            picked = nn(z_pack[r], low[...]) * high[...]
            lines.append(jnp.sum(picked, axis=0, keepdims=True) * (column * own))
        gram_out[pl.ds(pl.multiple_of(block * 8, 8), 8), :] = jnp.concatenate(lines, axis=0)

    @pl.loop(1, scens)
    def _(d):
        arrived(mine_in.at[scen_peer(d)], pb_r.at[scen_peer(d)])

    def add_mine(d, carry):
        return carry + mine_in[scen_peer(d)]

    last = lax.fori_loop(1, scens, add_mine, mine_part[s])
    last = pltpu.roll(jnp.broadcast_to(last, (8, 128)), (128 - rows * (p % 8)) % 128, 1)
    rhs_out[...] = last[0:1] * own_scale

    arrived(parts_in.at[pl.ds(0, path_devices - 1)], pa_s)

    @pl.loop(1, scens)
    def _(d):
        t = scen_peer(d)
        full_copy(t).wait_send()
        mine_copy(t).wait_send()

    @pl.loop(0, scens)
    def _(t):
        forward_copy(t).wait_send()


def finish_kernel(values, coef, gram, rhs, values_out, coef_out, gram_out, rhs_out):
    values_out[...] = values[...]
    coef_out[...] = coef[...]
    gram_out[...] = gram[...]
    rhs_out[...] = rhs[:, 0 : rhs_out.shape[1]]


VMEM = pl.BlockSpec(memory_space=pltpu.VMEM)
SMEM = pl.BlockSpec(memory_space=pltpu.SMEM)
DMA = pltpu.SemaphoreType.DMA


def on_device(
    states, exercise_dates, itm_mask, surrender, terminal, discount, ls_table, proxy_table
):
    scens, path_devices = lax.axis_size("scen"), lax.axis_size("path")
    paths = states.shape[3]
    terms, proxy_terms = ls_table.shape[0], proxy_table.shape[0]
    devices = scens * path_devices
    seats = path_devices // 2
    own_rows = proxy_terms // devices
    columns = proxy_table.T
    rows = 384 // seats
    buffer = pltpu.VMEM
    tiles = proxy_terms // 128

    values, coefficients, proxy_gram, proxy_rhs = pl.pallas_call(
        functools.partial(step_kernel, path_devices, scens),
        out_shape=(
            jax.ShapeDtypeStruct((1, paths), F32),
            jax.ShapeDtypeStruct((2, terms), F32),
            jax.ShapeDtypeStruct((own_rows, proxy_terms), F32),
            jax.ShapeDtypeStruct((1, 128), F32),
        ),
        in_specs=[SMEM] * 2 + [pl.BlockSpec(memory_space=pl.ANY)] + [VMEM] * 6,
        out_specs=[VMEM] * 4,
        scratch_shapes=[
            buffer((32, paths), F32), buffer((32, paths), F32),
            buffer((SIDE, paths), F32), buffer((SIDE, paths), F32),
            buffer((SIDE, SIDE), F32),
            buffer((2, terms, paths), BF16),
            buffer((2, seats, rows, 128), F32),
            buffer((seats, rows, 128), F32), buffer((seats, rows, 128), F32), buffer((seats, rows, 128), F32),
            buffer((2, seats, rows, 128), F32),
            buffer((1, terms), F32), buffer((path_devices, 1, terms), F32),
            buffer((1, terms), F32), buffer((path_devices, 1, terms), F32),
            buffer((2, terms, terms), F32), buffer((8, 8, 128), F32), buffer((8, 128), F32),
            buffer((2, scens, CHUNK, 128), F32),
            buffer((scens, CHUNK, 128), F32), buffer((scens, CHUNK, 128), F32), buffer((scens, CHUNK, 128), F32),
            buffer((CHUNK, 128), F32),
            buffer((seats, CHUNK // seats, 128), F32), buffer((seats, CHUNK // seats, 128), F32),
            buffer((seats, CHUNK // seats, 128), F32),
            buffer((2, scens, CHUNK, 128), F32),
            buffer((terms, 8), jnp.int32),
            pltpu.SMEM((8, 128), jnp.int32),
            buffer((4, 3, PAIRS, SIDE), BF16),
            buffer((own_rows, PAIRS, SIDE), BF16), buffer((own_rows, PAIRS, SIDE), BF16),
            buffer((own_rows, PAIRS, SIDE), BF16), buffer((own_rows, PAIRS, SIDE), BF16),
            buffer((own_rows, PAIRS, 256), BF16),
            buffer((256, proxy_terms), BF16), buffer((PAIRS, proxy_terms), F32),
            buffer((PAIRS, paths), F32), buffer((PAIRS, paths), F32),
            buffer((scens, tiles // scens, 1, 128), F32),
            buffer((path_devices, scens, 1, 128), F32),
            buffer((scens, 1, 128), F32), buffer((scens, 1, 128), F32),
            DMA, DMA,
            DMA, DMA, DMA, DMA, DMA, DMA,
            DMA, DMA, DMA, DMA,
            DMA((scens,)), DMA((scens,)),
            DMA((scens,)), DMA((scens,)), DMA((seats,)), DMA((seats,)), DMA((seats,)), DMA((seats,)),
            DMA((scens,)), DMA((scens,)), DMA((scens,)), DMA((scens,)),
            DMA, DMA,
            DMA((scens,)), DMA((scens,)), DMA,
        ],
        compiler_params=pltpu.CompilerParams(collective_id=0, has_side_effects=True),
        name="step",
    )(
        exercise_dates[0], discount[0], columns, states[0], itm_mask[0], surrender.transpose(1, 0, 2), terminal,
        ls_table.T, columns,
    )
    values, coefficients, proxy_gram, proxy_rhs = pl.pallas_call(
        finish_kernel,
        out_shape=(
            jax.ShapeDtypeStruct((1, paths), F32),
            jax.ShapeDtypeStruct((2, terms), F32),
            jax.ShapeDtypeStruct((own_rows, proxy_terms), F32),
            jax.ShapeDtypeStruct((1, own_rows), F32),
        ),
        in_specs=[VMEM] * 4,
        out_specs=[VMEM] * 4,
        name="finish",
    )(values, coefficients, proxy_gram, proxy_rhs)
    return (values, coefficients[None], proxy_gram, proxy_rhs[0])


def solution(mesh):
    placed = (
        P("scen", None, None, "path"),
        P("scen", None),
        P("scen", None, "path"),
        P("scen", None, "path"),
        P("scen", "path"),
        P("scen", None),
        P(),
        P(),
    )
    return jax.shard_map(
        on_device,
        mesh=mesh,
        in_specs=placed,
        out_specs=(
            P("scen", "path"),
            P("scen", None, None),
            P(("scen", "path"), None),
            P(("scen", "path")),
        ),
        check_vma=False,
    )
```

```python
import functools

import jax
import jax.numpy as jnp
from jax import lax
from jax.experimental import pallas as pl
from jax.experimental.pallas import tpu as pltpu
from jax.sharding import PartitionSpec as P

MESH = pl.DeviceIdType.MESH
HI = lax.Precision.HIGHEST
F32, BF16 = jnp.float32, jnp.bfloat16
ROOT_HALF = 0.7071067811865476
SIDE = 640
CHUNK = 400
PAIRS = 96
STEP = 32


def nt(a, b):
    return lax.dot_general(a, b, (((1,), (1,)), ((), ())), preferred_element_type=F32)


def nn(a, b):
    return jnp.dot(a, b, preferred_element_type=F32)


def halves(x):
    high = x.astype(BF16)
    return high, (x - high.astype(F32)).astype(BF16)


def three_rows(x):
    high = x.astype(BF16).astype(F32)
    rest = x - high
    mid = rest.astype(BF16).astype(F32)
    sub = lax.broadcasted_iota(jnp.int32, (8, x.shape[1]), 0)
    low = rest - mid
    return jnp.where(
        sub == 0, high, jnp.where(sub == 1, mid, jnp.where(sub == 2, low, 0.0))
    ).astype(BF16)


def add_rows(x):
    return x[0:1] + x[1:2] + x[2:3]


def products(factors, pair_a, pair_b, out, levels):
    count = levels * levels
    for i in range(levels):
        for j in range(levels):
            row = i * levels + j
            pair_a[row : row + 1, :] = factors[0][i] * factors[1][j]
            pair_b[row : row + 1, :] = factors[2][i] * factors[3][j]
    for i in range(count):
        out[i * count : (i + 1) * count, :] = pair_a[i : i + 1, :] * pair_b[0:count, :]


def sweep_small(e, n):
    def at(i, j):
        return e[min(i, j), max(i, j)]

    for k in range(0, n, 2):
        p, q, s = e[k, k], e[k, k + 1], e[k + 1, k + 1]
        w = 1.0 / (p * s - q * q)
        pw, qw, sw = p * w, q * w, s * w
        others = [i for i in range(n) if i not in (k, k + 1)]
        r0 = {i: at(k, i) for i in others}
        r1 = {i: at(k + 1, i) for i in others}
        x0 = {i: sw * r0[i] - qw * r1[i] for i in others}
        x1 = {i: pw * r1[i] - qw * r0[i] for i in others}
        for i in others:
            for j in others:
                if i <= j:
                    e[i, j] = e[i, j] - (r0[i] * x0[j] + r1[i] * x1[j])
        for i in others:
            e[min(i, k), max(i, k)] = x0[i]
            e[min(i, k + 1), max(i, k + 1)] = x1[i]
        e[k, k], e[k, k + 1], e[k + 1, k + 1] = -sw, qw, -pw
    return e


def tree_sum(terms):
    while len(terms) > 1:
        terms = [terms[t] + terms[t + 1] for t in range(0, len(terms), 2)]
    return terms[0]


def leaf(a, e_ref, r_ref):
    lane = lax.broadcasted_iota(jnp.int32, (STEP, 128), 1)
    lane8 = lax.broadcasted_iota(jnp.int32, (8, 128), 1)
    sub8 = lax.broadcasted_iota(jnp.int32, (8, 128), 0)
    half = lane - lane % 64
    in_half = lane8 % 64
    for o in range(0, STEP, 8):
        cols = [jnp.take_along_axis(a, half + (o + j), axis=1) for j in range(8)]
        r_ref[...] = a[o : o + 8, :]
        for j in range(8):
            e_ref[j] = cols[j][o : o + 8, :]
        e = {(i, j): e_ref[j, pl.ds(i, 8, stride=0), :] for i in range(8) for j in range(i, 8)}
        e = sweep_small(e, 8)
        rows = [r_ref[pl.ds(i, 8, stride=0), :] for i in range(8)]
        xs = []
        for i in range(8):
            entries = [e[min(i, j), max(i, j)] for j in range(8)]
            x = -tree_sum([entries[j] * rows[j] for j in range(8)])
            for j in range(8):
                x = jnp.where(in_half == o + j, entries[j], x)
            xs.append(x)
        tile = xs[0]
        for i in range(1, 8):
            tile = jnp.where(sub8 == i, xs[i], tile)
        inside = (in_half >= o) & (in_half < o + 8)
        tiles = []
        for t in range(0, STEP, 8):
            if t == o:
                tiles.append(tile)
            else:
                base = jnp.where(inside, 0.0, a[t : t + 8, :])
                tiles.append(base - tree_sum([cols[j][t : t + 8, :] * xs[j] for j in range(8)]))
        a = jnp.concatenate(tiles, axis=0)
    return a


def thirds(x):
    high = x.astype(BF16).astype(F32)
    rest = x - high
    mid = rest.astype(BF16).astype(F32)
    return high, mid, rest - mid


def pack_left(x):
    a, b, c = thirds(x)
    lane = lax.broadcasted_iota(jnp.int32, x.shape, 1)
    first = jnp.where(lane < 64, jnp.where(lane < 32, a, pltpu.roll(a, 32, 1)),
                      jnp.where(lane < 96, pltpu.roll(b, 64, 1), pltpu.roll(b, 96, 1)))
    second = jnp.where(lane < 32, a, jnp.where(lane < 64, pltpu.roll(c, 32, 1), 0.0))
    return jnp.concatenate([first, second], axis=1).astype(BF16)


def pack_right(x):
    a, b, c = thirds(x)
    zero = jnp.zeros_like(a)
    return jnp.concatenate([a, b, a, b, c, a, zero, zero], axis=0).astype(BF16)


def eliminate(a_ref, e_ref, r_ref, start, stop):
    n = a_ref.shape[1]
    lane = lax.broadcasted_iota(jnp.int32, (STEP, n), 1)
    lane1 = lax.broadcasted_iota(jnp.int32, (STEP, 128), 1)
    lane2 = lax.broadcasted_iota(jnp.int32, (n - STEP, n), 1)

    def body(k, _):
        first = [a_ref[d, 0:STEP, 0:128] for d in range(2)]
        lefts = [pack_left(a_ref[d, STEP:, 0:128]) for d in range(2)]
        rights = [pack_right(a_ref[d, 0:STEP, :]) for d in range(2)]
        both = leaf(jnp.where(lane1 < 64, first[0], pltpu.roll(first[1], 64, 1)), e_ref, r_ref)
        for d, neg in enumerate((both, pltpu.roll(both, 64, 1))):
            rest = a_ref[d, STEP:, :]
            x = nn(pack_left(neg), rights[d])
            xt = jnp.where(lane < STEP, jnp.concatenate([neg, neg], axis=1), -x)
            new = jnp.where(lane2 < STEP, 0.0, rest) - nn(lefts[d], pack_right(xt))
            a_ref[d, 0 : n - STEP, :] = pltpu.roll(new, n - STEP, 1)
            a_ref[d, n - STEP :, :] = pltpu.roll(xt, n - STEP, 1)
        return 0

    lax.fori_loop(start, stop, body, 0)


def arrived(buffer, sem):
    pltpu.make_async_copy(buffer, buffer, sem).wait()


def step_kernel(
    path_devices, scens,
    dates, disc, table_any, states, mask, surrender, terminal, ls_columns, table,
    values_out, coef_out, gram_out, rhs_out,
    pair_a, pair_b, left, right, whole, design, gram, gram_half, gram_acc, gram_in, gram_all,
    rhs_own, rhs_in, rhs0_own, rhs0_in, a_ref, e_ref, r_ref,
    mom, mom_half, mom_acc, x_in, x_sum, seat_out, seat_in, seat_all, full, ls_table, mine, pattern, pick_l, pick_r, y_high, y_low, z_pack,
    low, high, left3, right3, parts, parts_in, mine_part, mine_in,
    gh_s, gh_r, g_s, g_r, ga_s, ga_r, gf_s, gf_r, rhs_s, rhs_r, rhs0_s, rhs0_r,
    half_s, half_r, xr_s, xr_r, sr_s, sr_r, sa_s, sa_r, xa_s, xa_r, fw_s, fw_r, pa_s, pa_r, pb_s, pb_r, own_s,
):
    paths = terminal.shape[1]
    terms = ls_columns.shape[1]
    s, p = lax.axis_index("scen"), lax.axis_index("path")
    core, seat = p % 2, p // 2
    seats = path_devices // 2
    rows = gram_out.shape[0]
    index = s * path_devices + p
    first_own = rows * (index % (128 // rows))
    total_paths = paths * path_devices
    scale = 1.0 / total_paths
    own_scale = 1.0 / (total_paths * scens)
    partner = (s, seat * 2 + 1 - core)

    def path_peer(d):
        return (p + d) % path_devices

    def seat_peer(d):
        return (seat + d) % seats

    def scen_peer(d):
        return (s + d) % scens

    def seat_id(j):
        return (s, j * 2 + core)

    def send(src, dst, send_sem, recv_sem, target):
        return pltpu.make_async_remote_copy(
            src_ref=src, dst_ref=dst, send_sem=send_sem, recv_sem=recv_sem,
            device_id=target, device_id_type=MESH)

    def gram_half_copy():
        return send(gram.at[1 - core], gram_half, gh_s, gh_r, partner)

    def gram_copy(j):
        return send(gram_acc.at[j], gram_in.at[seat], g_s, g_r, seat_id(j))

    def gram_all_copy(j):
        block = gram_all.at[core, seat]
        return send(block, block, ga_s, ga_r, seat_id(j))

    def gram_forward():
        return send(gram_all.at[core], gram_all.at[core], gf_s, gf_r, partner)

    def rhs_copy(q):
        return send(rhs_own, rhs_in.at[p], rhs_s, rhs_r, (s, q))

    def rhs0_copy(q):
        return send(rhs0_own, rhs0_in.at[p], rhs0_s, rhs0_r, (s, q))

    def half_copy(t):
        return send(mom.at[1 - core, t], mom_half.at[t], half_s.at[t], half_r.at[t], partner)

    def x_copy(t):
        return send(mom_acc.at[t], x_in.at[s], xr_s.at[t], xr_r.at[s], (t, p))

    def seat_copy(j):
        return send(seat_out.at[j], seat_in.at[seat], sr_s, sr_r, seat_id(j))

    def seat_all_copy(j):
        block = seat_all.at[seat]
        return send(block, block, sa_s, sa_r, seat_id(j))

    def full_copy(t):
        block = full.at[core, s]
        return send(block, block, xa_s.at[t], xa_r.at[s], (t, p))

    def forward_copy(t):
        block = full.at[core, t]
        return send(block, block, fw_s.at[t], fw_r.at[t], partner)

    def part_copy(q):
        return send(parts.at[:, q // 8], parts_in.at[p], pa_s, pa_r, (s, q))

    def mine_copy(t):
        return send(mine_part.at[t], mine_in.at[s], pb_s.at[t], pb_r.at[s], (t, p))

    barrier = pltpu.get_barrier_semaphore()

    @pl.loop(1, path_devices)
    def _(d):
        pl.semaphore_signal(barrier, inc=1, device_id=(s, path_peer(d)), device_id_type=MESH)

    @pl.loop(1, scens)
    def _(d):
        pl.semaphore_signal(barrier, inc=1, device_id=(scen_peer(d), p), device_id_type=MESH)

    own_tile = pltpu.make_async_copy(
        table_any.at[:, pl.ds(pl.multiple_of(128 * (index // (128 // rows)), 128), 128)], mine, own_s
    )
    own_tile.start()
    ls_table[...] = ls_columns[...].T

    early = states[dates[0]]
    level_one = (early, states[dates[1]])
    level_two = [(u * u - 1.0) * ROOT_HALF for u in level_one]
    for top in range(0, terms, 32):
        t = ls_table[top : top + 32, :]
        result = [None, None]
        for v in range(8):
            degree = jnp.broadcast_to(t[:, v : v + 1], (32, 128))
            is_one = jnp.concatenate([degree == 1] * (paths // 128), axis=1)
            is_two = jnp.concatenate([degree == 2] * (paths // 128), axis=1)
            for d in range(2):
                level = jnp.where(
                    is_one,
                    level_one[d][v : v + 1, :],
                    jnp.where(is_two, level_two[d][v : v + 1, :], 1.0),
                )
                result[d] = level if v == 0 else result[d] * level
        for d in range(2):
            design[d, top : top + 32, :] = result[d].astype(BF16)
    for backward in (1, 0):
        live = design[backward]
        weighted = live * mask[backward : backward + 1, :].astype(F32).astype(BF16)
        g = nt(weighted, live)
        blocks = jnp.concatenate([g[0:128, 0:128], g[128:256, 0:128], g[128:256, 128:256]], axis=0)
        gram[backward] = blocks.reshape(gram.shape[1:])
        if backward == 1:
            rhs_own[...] = add_rows(nt(three_rows(disc[1] * terminal[...]), weighted))

    pl.semaphore_wait(barrier, path_devices - 1 + scens - 1)
    gram_half_copy().start()

    g = early * early - 1.0
    h = g * ROOT_HALF
    one = jnp.ones((1, paths), F32)

    def five(v):
        x, y = early[v : v + 1, :], g[v : v + 1, :]
        return [one, x, y, x * y, y * y]

    for side, first in ((left, 0), (right, 4)):
        side[624:SIDE, :] = jnp.zeros((SIDE - 624, paths), F32)
        products([five(first + v) for v in range(4)], pair_a, pair_b, side, 5)

    gram_half_copy().wait()
    gram_acc[...] = gram[core] + gram_half[...]

    @pl.loop(1, seats)
    def _(d):
        gram_copy(seat_peer(d)).start()

    lh, ll = halves(left[...])
    rh, rl = halves(right[...])
    moments = nt(lh, rh) + nt(lh, rl) + nt(ll, rh)
    for k in range(SIDE // 128):
        low_row = k * SIDE
        while low_row < (k + 1) * SIDE:
            c = low_row // CHUNK
            top_row = min((k + 1) * SIDE, (c + 1) * CHUNK)
            mom[c // scens, c % scens, low_row - c * CHUNK : top_row - c * CHUNK, :] = moments[
                low_row - k * SIDE : top_row - k * SIDE, k * 128 : (k + 1) * 128
            ]
            low_row = top_row

    @pl.loop(1, scens + 1)
    def _(d):
        half_copy(scen_peer(d)).start()

    @pl.loop(1, path_devices)
    def _(d):
        rhs_copy(path_peer(d)).start()

    arrived(gram_in.at[pl.ds(0, seats - 1)], g_r)

    def add_gram(d, carry):
        return carry + gram_in[seat_peer(d)]

    gram_all[core, seat] = lax.fori_loop(1, seats, add_gram, gram_acc[seat])

    @pl.loop(1, seats)
    def _(d):
        gram_all_copy(seat_peer(d)).start()


    @pl.loop(1, scens)
    def _(d):
        t = scen_peer(d)
        arrived(mom_half.at[t], half_r.at[t])
        mom_acc[t] = mom[core, t] + mom_half[t]
        x_copy(t).start()

    arrived(mom_half.at[s], half_r.at[s])
    mom_acc[s] = mom[core, s] + mom_half[s]

    row = lax.broadcasted_iota(jnp.int32, high.shape, 0)
    for first, is_low in ((0, True), (4, False)):
        t = [table[first + v : first + v + 1, :] for v in range(4)]
        code = ((t[0] * 3 + t[1]) * 3 + t[2]) * 3 + t[3]
        hot = jnp.where(row == code, 1.0, 0.0)
        if is_low:
            low[0:PAIRS, :] = hot.astype(BF16)
            low[PAIRS:128, :] = jnp.zeros((128 - PAIRS, hot.shape[1]), BF16)
            low[128 : 128 + PAIRS, :] = hot.astype(BF16)
            low[128 + PAIRS : 256, :] = jnp.zeros((128 - PAIRS, hot.shape[1]), BF16)
        else:
            high[...] = hot

    arrived(gram_all.at[core, pl.ds(0, seats - 1)], ga_r)
    gram_forward().start()

    arrived(gram_all.at[1 - core], gf_r)

    ri = lax.broadcasted_iota(jnp.int32, (128, 128), 0)
    ci = lax.broadcasted_iota(jnp.int32, (128, 128), 1)
    ridge = jnp.where(ri == ci, 0.05, 0.0)
    for d in range(2):
        stack = gram_all[d].reshape(384, 128) * scale
        corner = stack[128:256, :]
        a_ref[d, 0:128, 0:128] = stack[0:128, :] + ridge
        a_ref[d, 128:256, 0:128] = corner
        a_ref[d, 0:128, 128:256] = corner.T
        a_ref[d, 128:256, 128:256] = stack[256:384, :] + ridge
    steps = terms // STEP
    eliminate(a_ref, e_ref, r_ref, 0, steps // 4)

    @pl.loop(1, scens)
    def _(d):
        arrived(x_in.at[scen_peer(d)], xr_r.at[scen_peer(d)])

    x_sum[...] = lax.fori_loop(1, scens, lambda d, carry: carry + x_in[scen_peer(d)], mom_acc[s])
    own_part = CHUNK // seats
    for j in range(seats):
        seat_out[j] = x_sum[j * own_part : (j + 1) * own_part, :]

    @pl.loop(1, seats)
    def _(d):
        seat_copy(seat_peer(d)).start()

    eliminate(a_ref, e_ref, r_ref, steps // 4, steps // 2)

    arrived(seat_in.at[pl.ds(0, seats - 1)], sr_r)

    seat_all[seat] = lax.fori_loop(
        1, seats, lambda d, carry: carry + seat_in[seat_peer(d)], seat_out[seat]
    )

    @pl.loop(1, seats)
    def _(d):
        seat_all_copy(seat_peer(d)).start()

    eliminate(a_ref, e_ref, r_ref, steps // 2, 3 * steps // 4)

    arrived(seat_all.at[pl.ds(0, seats - 1)], sa_r)

    for j in range(seats):
        full[core, s, j * own_part : (j + 1) * own_part, :] = seat_all[j]

    @pl.loop(1, scens)
    def _(d):
        full_copy(scen_peer(d)).start()

    forward_copy(s).start()
    eliminate(a_ref, e_ref, r_ref, 3 * steps // 4, steps)

    arrived(rhs_in.at[pl.ds(0, path_devices - 1)], rhs_r)

    def add_rhs(d, carry):
        return carry + rhs_in[path_peer(d)]

    rhs = lax.fori_loop(1, path_devices, add_rhs, rhs_own[...]) * scale
    coef = -jnp.dot(
        jnp.broadcast_to(rhs, (8, terms)), a_ref[1], precision=HI, preferred_element_type=F32
    )[0:1]
    coef_out[1:2, :] = coef
    continuation = add_rows(nn(three_rows(coef), design[1]))
    payoff = surrender[dates[1]]
    values = disc[1] * terminal[...]
    values = jnp.where(mask[1:2, :] > 0, jnp.maximum(payoff, continuation), values)
    values = disc[0] * values
    weighted = design[0] * mask[0:1, :].astype(F32).astype(BF16)
    rhs0_own[...] = add_rows(nt(three_rows(values), weighted))

    @pl.loop(1, path_devices)
    def _(d):
        rhs0_copy(path_peer(d)).start()

    for out, first in ((left3, 0), (right3, 4)):
        out[80:PAIRS, :] = jnp.zeros((PAIRS - 80, paths), F32)
        levels = [
            [one, early[first + v : first + v + 1, :], h[first + v : first + v + 1, :]]
            for v in range(4)
        ]
        products(levels, pair_a, pair_b, out, 3)
    prow = lax.broadcasted_iota(jnp.int32, (PAIRS, 1), 0)
    plane = lax.broadcasted_iota(jnp.int32, (1, SIDE), 1)
    for v, (three, five_) in enumerate(((27, 125), (9, 25), (3, 5), (1, 1))):
        b = jnp.where(prow < 81, (prow // three) % 3, -9)
        m = jnp.where(plane < 625, (plane // five_) % 5, -20)
        b, m = jnp.broadcast_to(b, (PAIRS, SIDE)), jnp.broadcast_to(m, (PAIRS, SIDE))
        ones = ((b == 0) & (m == 1)) | ((b == 1) & ((m == 0) | (m == 2))) | ((b == 2) & (m == 3))
        pattern[v, 0] = jnp.where(m == b, 1.0, 0.0).astype(BF16)
        pattern[v, 1] = jnp.where(ones, 1.0, 0.0).astype(BF16)
        pattern[v, 2] = jnp.where(m == b + 2, 1.0, 0.0).astype(BF16)

    own_tile.wait()

    @pl.loop(0, rows)
    def _(r):
        def pattern_of(first):
            result = None
            for v in range(4):
                block = pattern[v, mine[first + v, first_own + r]]
                result = block if result is None else result * block
            return result

        pick_l[r] = pattern_of(0)
        pick_r[r] = pattern_of(4)

    arrived(gram_in.at[pl.ds(0, seats - 1)], g_s)
    arrived(gram_in.at[pl.ds(0, seats - 1)], ga_s)
    arrived(gram_all.at[core], gf_s)
    arrived(rhs_in.at[pl.ds(0, path_devices - 1)], rhs_s)

    arrived(seat_in.at[pl.ds(0, seats - 1)], sr_s)
    arrived(seat_in.at[pl.ds(0, seats - 1)], sa_s)

    @pl.loop(1, scens)
    def _(d):
        x_copy(scen_peer(d)).wait_send()

    @pl.loop(0, scens)
    def _(t):
        half_copy(t).wait_send()

    @pl.loop(1, scens)
    def _(d):
        t = scen_peer(d)
        arrived(full.at[core, t], xa_r.at[t])
        forward_copy(t).start()

    arrived(rhs0_in.at[pl.ds(0, path_devices - 1)], rhs0_r)
    arrived(rhs0_in.at[pl.ds(0, path_devices - 1)], rhs0_s)

    def add_rhs0(d, carry):
        return carry + rhs0_in[path_peer(d)]

    rhs = lax.fori_loop(1, path_devices, add_rhs0, rhs0_own[...]) * scale
    coef = -jnp.dot(
        jnp.broadcast_to(rhs, (8, terms)), a_ref[0], precision=HI, preferred_element_type=F32
    )[0:1]
    coef_out[0:1, :] = coef
    continuation = add_rows(nn(three_rows(coef), design[0]))
    payoff = surrender[dates[0]]
    final = jnp.where(mask[0:1, :] > 0, jnp.maximum(payoff, continuation), values)
    values_out[...] = final

    rounded = final.astype(BF16).astype(F32)
    lh, ll = halves(left3[...] * rounded)
    rh, rl = halves(right3[...])
    wh, wl = halves(nt(rh, lh) + nt(rh, ll) + nt(rl, lh))
    hot = low[0:PAIRS, :]
    picked = jnp.sum((nn(wh, hot) + nn(wl, hot)) * high[...], axis=0, keepdims=True)
    for t in range(parts.shape[0]):
        for q in range(parts.shape[1]):
            k = (t * parts.shape[1] + q) * 128
            parts[t, q] = picked[:, k : k + 128]

    @pl.loop(1, path_devices)
    def _(d):
        part_copy(path_peer(d)).start()

    @pl.loop(0, scens)
    def _(t):
        arrived(full.at[1 - core, t], fw_r.at[t])

    for k in range(SIDE // 128):
        low_row = k * SIDE
        while low_row < (k + 1) * SIDE:
            c = low_row // CHUNK
            top_row = min((k + 1) * SIDE, (c + 1) * CHUNK)
            whole[low_row - k * SIDE : top_row - k * SIDE, k * 128 : (k + 1) * 128] = full[
                c // scens, c % scens, low_row - c * CHUNK : top_row - c * CHUNK, :
            ]
            low_row = top_row
    mh, ml = halves(whole[...])
    picks = pick_l[...].reshape(rows * PAIRS, SIDE)
    yh, yl = halves(nn(picks, mh) + nn(picks, ml))
    y_high[...] = yh.reshape(y_high.shape)
    y_low[...] = yl.reshape(y_low.shape)

    def second_product(r):
        zh, zl = halves(nt(pick_r[r], y_high[r]) + nt(pick_r[r], y_low[r]))
        z_pack[r, :, 0:PAIRS] = zh
        z_pack[r, :, 128 : 128 + PAIRS] = zl

    z_pack[...] = jnp.zeros(z_pack.shape, BF16)
    pl.loop(0, rows // 2)(second_product)

    arrived(parts_in.at[pl.ds(0, path_devices - 1)], pa_r)

    def add_part(d, carry):
        return carry + parts_in[path_peer(d)]

    mine_part[...] = lax.fori_loop(1, path_devices, add_part, parts[:, p // 8])

    @pl.loop(1, scens)
    def _(d):
        mine_copy(scen_peer(d)).start()

    pl.loop(rows // 2, rows)(second_product)

    column = None
    for v in range(8):
        factor = jnp.where(table[v : v + 1, :] == 2, ROOT_HALF, 1.0)
        column = factor if column is None else column * factor

    @pl.loop(0, rows // 8)
    def _(block):
        lines = []
        for k in range(8):
            r = block * 8 + k
            own = own_scale
            for v in range(8):
                own = own * jnp.where(mine[v, first_own + r] == 2, ROOT_HALF, 1.0)
            picked = nn(z_pack[r], low[...]) * high[...]
            lines.append(jnp.sum(picked, axis=0, keepdims=True) * (column * own))
        gram_out[pl.ds(pl.multiple_of(block * 8, 8), 8), :] = jnp.concatenate(lines, axis=0)

    @pl.loop(1, scens)
    def _(d):
        arrived(mine_in.at[scen_peer(d)], pb_r.at[scen_peer(d)])

    def add_mine(d, carry):
        return carry + mine_in[scen_peer(d)]

    last = lax.fori_loop(1, scens, add_mine, mine_part[s])
    last = pltpu.roll(jnp.broadcast_to(last, (8, 128)), (128 - rows * (p % 8)) % 128, 1)
    rhs_out[...] = last[0:1] * own_scale

    arrived(parts_in.at[pl.ds(0, path_devices - 1)], pa_s)

    @pl.loop(1, scens)
    def _(d):
        t = scen_peer(d)
        full_copy(t).wait_send()
        mine_copy(t).wait_send()

    @pl.loop(0, scens)
    def _(t):
        forward_copy(t).wait_send()


def finish_kernel(values, coef, gram, rhs, values_out, coef_out, gram_out, rhs_out):
    values_out[...] = values[...]
    coef_out[...] = coef[...]
    gram_out[...] = gram[...]
    rhs_out[...] = rhs[:, 0 : rhs_out.shape[1]]


VMEM = pl.BlockSpec(memory_space=pltpu.VMEM)
SMEM = pl.BlockSpec(memory_space=pltpu.SMEM)
DMA = pltpu.SemaphoreType.DMA


def on_device(
    states, exercise_dates, itm_mask, surrender, terminal, discount, ls_table, proxy_table
):
    scens, path_devices = lax.axis_size("scen"), lax.axis_size("path")
    paths = states.shape[3]
    terms, proxy_terms = ls_table.shape[0], proxy_table.shape[0]
    devices = scens * path_devices
    seats = path_devices // 2
    own_rows = proxy_terms // devices
    columns = proxy_table.T
    rows = 384 // seats
    buffer = pltpu.VMEM
    tiles = proxy_terms // 128

    values, coefficients, proxy_gram, proxy_rhs = pl.pallas_call(
        functools.partial(step_kernel, path_devices, scens),
        out_shape=(
            jax.ShapeDtypeStruct((1, paths), F32),
            jax.ShapeDtypeStruct((2, terms), F32),
            jax.ShapeDtypeStruct((own_rows, proxy_terms), F32),
            jax.ShapeDtypeStruct((1, 128), F32),
        ),
        in_specs=[SMEM] * 2 + [pl.BlockSpec(memory_space=pl.ANY)] + [VMEM] * 6,
        out_specs=[VMEM] * 4,
        scratch_shapes=[
            buffer((32, paths), F32), buffer((32, paths), F32),
            buffer((SIDE, paths), F32), buffer((SIDE, paths), F32),
            buffer((SIDE, SIDE), F32),
            buffer((2, terms, paths), BF16),
            buffer((2, seats, rows, 128), F32),
            buffer((seats, rows, 128), F32), buffer((seats, rows, 128), F32), buffer((seats, rows, 128), F32),
            buffer((2, seats, rows, 128), F32),
            buffer((1, terms), F32), buffer((path_devices, 1, terms), F32),
            buffer((1, terms), F32), buffer((path_devices, 1, terms), F32),
            buffer((2, terms, terms), F32), buffer((8, 8, 128), F32), buffer((8, 128), F32),
            buffer((2, scens, CHUNK, 128), F32),
            buffer((scens, CHUNK, 128), F32), buffer((scens, CHUNK, 128), F32), buffer((scens, CHUNK, 128), F32),
            buffer((CHUNK, 128), F32),
            buffer((seats, CHUNK // seats, 128), F32), buffer((seats, CHUNK // seats, 128), F32),
            buffer((seats, CHUNK // seats, 128), F32),
            buffer((2, scens, CHUNK, 128), F32),
            buffer((terms, 8), jnp.int32),
            pltpu.SMEM((8, 128), jnp.int32),
            buffer((4, 3, PAIRS, SIDE), BF16),
            buffer((own_rows, PAIRS, SIDE), BF16), buffer((own_rows, PAIRS, SIDE), BF16),
            buffer((own_rows, PAIRS, SIDE), BF16), buffer((own_rows, PAIRS, SIDE), BF16),
            buffer((own_rows, PAIRS, 256), BF16),
            buffer((256, proxy_terms), BF16), buffer((PAIRS, proxy_terms), F32),
            buffer((PAIRS, paths), F32), buffer((PAIRS, paths), F32),
            buffer((scens, tiles // scens, 1, 128), F32),
            buffer((path_devices, scens, 1, 128), F32),
            buffer((scens, 1, 128), F32), buffer((scens, 1, 128), F32),
            DMA, DMA,
            DMA, DMA, DMA, DMA, DMA, DMA,
            DMA, DMA, DMA, DMA,
            DMA((scens,)), DMA((scens,)),
            DMA((scens,)), DMA((scens,)), DMA, DMA, DMA, DMA,
            DMA((scens,)), DMA((scens,)), DMA((scens,)), DMA((scens,)),
            DMA, DMA,
            DMA((scens,)), DMA((scens,)), DMA,
        ],
        compiler_params=pltpu.CompilerParams(collective_id=0, has_side_effects=True),
        name="step",
    )(
        exercise_dates[0], discount[0], columns, states[0], itm_mask[0], surrender.transpose(1, 0, 2), terminal,
        ls_table.T, columns,
    )
    values, coefficients, proxy_gram, proxy_rhs = pl.pallas_call(
        finish_kernel,
        out_shape=(
            jax.ShapeDtypeStruct((1, paths), F32),
            jax.ShapeDtypeStruct((2, terms), F32),
            jax.ShapeDtypeStruct((own_rows, proxy_terms), F32),
            jax.ShapeDtypeStruct((1, own_rows), F32),
        ),
        in_specs=[VMEM] * 4,
        out_specs=[VMEM] * 4,
        name="finish",
    )(values, coefficients, proxy_gram, proxy_rhs)
    return (values, coefficients[None], proxy_gram, proxy_rhs[0])


def solution(mesh):
    placed = (
        P("scen", None, None, "path"),
        P("scen", None),
        P("scen", None, "path"),
        P("scen", None, "path"),
        P("scen", "path"),
        P("scen", None),
        P(),
        P(),
    )
    return jax.shard_map(
        on_device,
        mesh=mesh,
        in_specs=placed,
        out_specs=(
            P("scen", "path"),
            P("scen", None, None),
            P(("scen", "path"), None),
            P(("scen", "path")),
        ),
        check_vma=False,
    )
```

```python
import functools

import jax
import jax.numpy as jnp
from jax import lax
from jax.experimental import pallas as pl
from jax.experimental.pallas import tpu as pltpu
from jax.sharding import PartitionSpec as P

MESH = pl.DeviceIdType.MESH
HI = lax.Precision.HIGHEST
F32, BF16 = jnp.float32, jnp.bfloat16
ROOT_HALF = 0.7071067811865476
SIDE = 640
CHUNK = 400
PAIRS = 96
STEP = 32


def nt(a, b):
    return lax.dot_general(a, b, (((1,), (1,)), ((), ())), preferred_element_type=F32)


def nn(a, b):
    return jnp.dot(a, b, preferred_element_type=F32)


def halves(x):
    high = x.astype(BF16)
    return high, (x - high.astype(F32)).astype(BF16)


def three_rows(x):
    high = x.astype(BF16).astype(F32)
    rest = x - high
    mid = rest.astype(BF16).astype(F32)
    sub = lax.broadcasted_iota(jnp.int32, (8, x.shape[1]), 0)
    low = rest - mid
    return jnp.where(
        sub == 0, high, jnp.where(sub == 1, mid, jnp.where(sub == 2, low, 0.0))
    ).astype(BF16)


def add_rows(x):
    return x[0:1] + x[1:2] + x[2:3]


def products(factors, pair_a, pair_b, out, levels):
    count = levels * levels
    for i in range(levels):
        for j in range(levels):
            row = i * levels + j
            pair_a[row : row + 1, :] = factors[0][i] * factors[1][j]
            pair_b[row : row + 1, :] = factors[2][i] * factors[3][j]
    for i in range(count):
        out[i * count : (i + 1) * count, :] = pair_a[i : i + 1, :] * pair_b[0:count, :]


def sweep_small(e, n):
    def at(i, j):
        return e[min(i, j), max(i, j)]

    for k in range(0, n, 2):
        p, q, s = e[k, k], e[k, k + 1], e[k + 1, k + 1]
        w = 1.0 / (p * s - q * q)
        pw, qw, sw = p * w, q * w, s * w
        others = [i for i in range(n) if i not in (k, k + 1)]
        r0 = {i: at(k, i) for i in others}
        r1 = {i: at(k + 1, i) for i in others}
        x0 = {i: sw * r0[i] - qw * r1[i] for i in others}
        x1 = {i: pw * r1[i] - qw * r0[i] for i in others}
        for i in others:
            for j in others:
                if i <= j:
                    e[i, j] = e[i, j] - (r0[i] * x0[j] + r1[i] * x1[j])
        for i in others:
            e[min(i, k), max(i, k)] = x0[i]
            e[min(i, k + 1), max(i, k + 1)] = x1[i]
        e[k, k], e[k, k + 1], e[k + 1, k + 1] = -sw, qw, -pw
    return e


def tree_sum(terms):
    while len(terms) > 1:
        terms = [terms[t] + terms[t + 1] for t in range(0, len(terms), 2)]
    return terms[0]


def leaf(a, e_ref, r_ref):
    lane = lax.broadcasted_iota(jnp.int32, (STEP, 128), 1)
    lane8 = lax.broadcasted_iota(jnp.int32, (8, 128), 1)
    sub8 = lax.broadcasted_iota(jnp.int32, (8, 128), 0)
    half = lane - lane % 64
    in_half = lane8 % 64
    for o in range(0, STEP, 8):
        cols = [jnp.take_along_axis(a, half + (o + j), axis=1) for j in range(8)]
        r_ref[...] = a[o : o + 8, :]
        for j in range(8):
            e_ref[j] = cols[j][o : o + 8, :]
        e = {(i, j): e_ref[j, pl.ds(i, 8, stride=0), :] for i in range(8) for j in range(i, 8)}
        e = sweep_small(e, 8)
        rows = [r_ref[pl.ds(i, 8, stride=0), :] for i in range(8)]
        xs = []
        for i in range(8):
            entries = [e[min(i, j), max(i, j)] for j in range(8)]
            x = -tree_sum([entries[j] * rows[j] for j in range(8)])
            for j in range(8):
                x = jnp.where(in_half == o + j, entries[j], x)
            xs.append(x)
        tile = xs[0]
        for i in range(1, 8):
            tile = jnp.where(sub8 == i, xs[i], tile)
        inside = (in_half >= o) & (in_half < o + 8)
        tiles = []
        for t in range(0, STEP, 8):
            if t == o:
                tiles.append(tile)
            else:
                base = jnp.where(inside, 0.0, a[t : t + 8, :])
                tiles.append(base - tree_sum([cols[j][t : t + 8, :] * xs[j] for j in range(8)]))
        a = jnp.concatenate(tiles, axis=0)
    return a


def thirds(x):
    high = x.astype(BF16).astype(F32)
    rest = x - high
    mid = rest.astype(BF16).astype(F32)
    return high, mid, rest - mid


def pack_left(x):
    a, b, c = thirds(x)
    lane = lax.broadcasted_iota(jnp.int32, x.shape, 1)
    first = jnp.where(lane < 64, jnp.where(lane < 32, a, pltpu.roll(a, 32, 1)),
                      jnp.where(lane < 96, pltpu.roll(b, 64, 1), pltpu.roll(b, 96, 1)))
    second = jnp.where(lane < 32, a, jnp.where(lane < 64, pltpu.roll(c, 32, 1), 0.0))
    return jnp.concatenate([first, second], axis=1).astype(BF16)


def pack_right(x):
    a, b, c = thirds(x)
    zero = jnp.zeros_like(a)
    return jnp.concatenate([a, b, a, b, c, a, zero, zero], axis=0).astype(BF16)


def eliminate(a_ref, e_ref, r_ref, start, stop):
    n = a_ref.shape[1]
    lane = lax.broadcasted_iota(jnp.int32, (STEP, n), 1)
    lane1 = lax.broadcasted_iota(jnp.int32, (STEP, 128), 1)
    lane2 = lax.broadcasted_iota(jnp.int32, (n - STEP, n), 1)

    def body(k, _):
        first = [a_ref[d, 0:STEP, 0:128] for d in range(2)]
        lefts = [pack_left(a_ref[d, STEP:, 0:128]) for d in range(2)]
        rights = [pack_right(a_ref[d, 0:STEP, :]) for d in range(2)]
        both = leaf(jnp.where(lane1 < 64, first[0], pltpu.roll(first[1], 64, 1)), e_ref, r_ref)
        for d, neg in enumerate((both, pltpu.roll(both, 64, 1))):
            rest = a_ref[d, STEP:, :]
            x = nn(pack_left(neg), rights[d])
            xt = jnp.where(lane < STEP, jnp.concatenate([neg, neg], axis=1), -x)
            new = jnp.where(lane2 < STEP, 0.0, rest) - nn(lefts[d], pack_right(xt))
            a_ref[d, 0 : n - STEP, :] = pltpu.roll(new, n - STEP, 1)
            a_ref[d, n - STEP :, :] = pltpu.roll(xt, n - STEP, 1)
        return 0

    lax.fori_loop(start, stop, body, 0)


def arrived(buffer, sem):
    pltpu.make_async_copy(buffer, buffer, sem).wait()


def step_kernel(
    path_devices, scens,
    dates, disc, table_any, states, mask, surrender, terminal, ls_columns, table,
    values_out, coef_out, gram_out, rhs_out,
    pair_a, pair_b, left, right, whole, design, gram, gram_half, gram_acc, gram_in, gram_all,
    rhs_own, rhs_in, rhs0_own, rhs0_in, a_ref, e_ref, r_ref,
    mom, mom_half, mom_acc, x_in, x_sum, seat_out, seat_in, seat_all, full, ls_table, mine, pattern, pick_l, pick_r, y_high, y_low, z_pack,
    low, high, left3, right3, parts, parts_in, mine_part, mine_in,
    gh_s, gh_r, g_s, g_r, ga_s, ga_r, gf_s, gf_r, rhs_s, rhs_r, rhs0_s, rhs0_r,
    half_s, half_r, xr_s, xr_r, sr_s, sr_r, sa_s, sa_r, xa_s, xa_r, fw_s, fw_r, pa_s, pa_r, pb_s, pb_r, own_s,
):
    paths = terminal.shape[1]
    terms = ls_columns.shape[1]
    s, p = lax.axis_index("scen"), lax.axis_index("path")
    core, seat = p % 2, p // 2
    seats = path_devices // 2
    rows = gram_out.shape[0]
    index = s * path_devices + p
    first_own = rows * (index % (128 // rows))
    total_paths = paths * path_devices
    scale = 1.0 / total_paths
    own_scale = 1.0 / (total_paths * scens)
    partner = (s, seat * 2 + 1 - core)

    def path_peer(d):
        return (p + d) % path_devices

    def seat_peer(d):
        return (seat + d) % seats

    def scen_peer(d):
        return (s + d) % scens

    def seat_id(j):
        return (s, j * 2 + core)

    def send(src, dst, send_sem, recv_sem, target):
        return pltpu.make_async_remote_copy(
            src_ref=src, dst_ref=dst, send_sem=send_sem, recv_sem=recv_sem,
            device_id=target, device_id_type=MESH)

    def gram_half_copy():
        return send(gram.at[1 - core], gram_half, gh_s, gh_r, partner)

    def gram_copy(j):
        return send(gram_acc.at[j], gram_in.at[seat], g_s, g_r, seat_id(j))

    def gram_all_copy(j):
        block = gram_all.at[core, seat]
        return send(block, block, ga_s, ga_r, seat_id(j))

    def gram_forward():
        return send(gram_all.at[core], gram_all.at[core], gf_s, gf_r, partner)

    def rhs_copy(q):
        return send(rhs_own, rhs_in.at[p], rhs_s, rhs_r, (s, q))

    def rhs0_copy(q):
        return send(rhs0_own, rhs0_in.at[p], rhs0_s, rhs0_r, (s, q))

    def half_copy(t):
        return send(mom.at[1 - core, t], mom_half.at[t], half_s.at[t], half_r.at[t], partner)

    def x_copy(t):
        return send(mom_acc.at[t], x_in.at[s], xr_s.at[t], xr_r.at[s], (t, p))

    def seat_copy(j):
        return send(seat_out.at[j], seat_in.at[seat], sr_s, sr_r, seat_id(j))

    def seat_all_copy(j):
        block = seat_all.at[seat]
        return send(block, block, sa_s, sa_r, seat_id(j))

    def full_copy(t):
        block = full.at[core, s]
        return send(block, block, xa_s.at[t], xa_r.at[s], (t, p))

    def forward_copy(t):
        block = full.at[core, t]
        return send(block, block, fw_s.at[t], fw_r.at[t], partner)

    def part_copy(q):
        return send(parts.at[:, q // 8], parts_in.at[p], pa_s, pa_r, (s, q))

    def mine_copy(t):
        return send(mine_part.at[t], mine_in.at[s], pb_s.at[t], pb_r.at[s], (t, p))

    barrier = pltpu.get_barrier_semaphore()

    @pl.loop(1, path_devices)
    def _(d):
        pl.semaphore_signal(barrier, inc=1, device_id=(s, path_peer(d)), device_id_type=MESH)

    @pl.loop(1, scens)
    def _(d):
        pl.semaphore_signal(barrier, inc=1, device_id=(scen_peer(d), p), device_id_type=MESH)

    own_tile = pltpu.make_async_copy(
        table_any.at[:, pl.ds(pl.multiple_of(128 * (index // (128 // rows)), 128), 128)], mine, own_s
    )
    own_tile.start()
    ls_table[...] = ls_columns[...].T

    early = states[dates[0]]
    level_one = (early, states[dates[1]])
    level_two = [(u * u - 1.0) * ROOT_HALF for u in level_one]
    for top in range(0, terms, 32):
        t = ls_table[top : top + 32, :]
        result = [None, None]
        for v in range(8):
            degree = jnp.broadcast_to(t[:, v : v + 1], (32, 128))
            is_one = jnp.concatenate([degree == 1] * (paths // 128), axis=1)
            is_two = jnp.concatenate([degree == 2] * (paths // 128), axis=1)
            for d in range(2):
                level = jnp.where(
                    is_one,
                    level_one[d][v : v + 1, :],
                    jnp.where(is_two, level_two[d][v : v + 1, :], 1.0),
                )
                result[d] = level if v == 0 else result[d] * level
        for d in range(2):
            design[d, top : top + 32, :] = result[d].astype(BF16)
    for backward in (1, 0):
        live = design[backward]
        weighted = live * mask[backward : backward + 1, :].astype(F32).astype(BF16)
        g = nt(weighted, live)
        blocks = jnp.concatenate([g[0:128, 0:128], g[128:256, 0:128], g[128:256, 128:256]], axis=0)
        gram[backward] = blocks.reshape(gram.shape[1:])
        if backward == 1:
            rhs_own[...] = add_rows(nt(three_rows(disc[1] * terminal[...]), weighted))

    pl.semaphore_wait(barrier, path_devices - 1 + scens - 1)
    gram_half_copy().start()

    g = early * early - 1.0
    h = g * ROOT_HALF
    one = jnp.ones((1, paths), F32)

    def five(v):
        x, y = early[v : v + 1, :], g[v : v + 1, :]
        return [one, x, y, x * y, y * y]

    for side, first in ((left, 0), (right, 4)):
        side[624:SIDE, :] = jnp.zeros((SIDE - 624, paths), F32)
        products([five(first + v) for v in range(4)], pair_a, pair_b, side, 5)

    gram_half_copy().wait()
    gram_acc[...] = gram[core] + gram_half[...]

    @pl.loop(1, seats)
    def _(d):
        gram_copy(seat_peer(d)).start()

    lh, ll = halves(left[...])
    rh, rl = halves(right[...])
    moments = nt(lh, rh) + nt(lh, rl) + nt(ll, rh)
    for k in range(SIDE // 128):
        low_row = k * SIDE
        while low_row < (k + 1) * SIDE:
            c = low_row // CHUNK
            top_row = min((k + 1) * SIDE, (c + 1) * CHUNK)
            mom[c // scens, c % scens, low_row - c * CHUNK : top_row - c * CHUNK, :] = moments[
                low_row - k * SIDE : top_row - k * SIDE, k * 128 : (k + 1) * 128
            ]
            low_row = top_row

    @pl.loop(1, scens + 1)
    def _(d):
        half_copy(scen_peer(d)).start()

    @pl.loop(1, path_devices)
    def _(d):
        rhs_copy(path_peer(d)).start()

    arrived(gram_in.at[pl.ds(0, seats - 1)], g_r)

    def add_gram(d, carry):
        return carry + gram_in[seat_peer(d)]

    gram_all[core, seat] = lax.fori_loop(1, seats, add_gram, gram_acc[seat])

    @pl.loop(1, seats)
    def _(d):
        gram_all_copy(seat_peer(d)).start()


    @pl.loop(1, scens)
    def _(d):
        t = scen_peer(d)
        arrived(mom_half.at[t], half_r.at[t])
        mom_acc[t] = mom[core, t] + mom_half[t]
        x_copy(t).start()

    arrived(mom_half.at[s], half_r.at[s])
    mom_acc[s] = mom[core, s] + mom_half[s]

    row = lax.broadcasted_iota(jnp.int32, high.shape, 0)
    for first, is_low in ((0, True), (4, False)):
        t = [table[first + v : first + v + 1, :] for v in range(4)]
        code = ((t[0] * 3 + t[1]) * 3 + t[2]) * 3 + t[3]
        hot = jnp.where(row == code, 1.0, 0.0)
        if is_low:
            low[0:PAIRS, :] = hot.astype(BF16)
            low[PAIRS:128, :] = jnp.zeros((128 - PAIRS, hot.shape[1]), BF16)
            low[128 : 128 + PAIRS, :] = hot.astype(BF16)
            low[128 + PAIRS : 256, :] = jnp.zeros((128 - PAIRS, hot.shape[1]), BF16)
        else:
            high[...] = hot

    arrived(gram_all.at[core, pl.ds(0, seats - 1)], ga_r)
    gram_forward().start()

    arrived(gram_all.at[1 - core], gf_r)

    ri = lax.broadcasted_iota(jnp.int32, (128, 128), 0)
    ci = lax.broadcasted_iota(jnp.int32, (128, 128), 1)
    ridge = jnp.where(ri == ci, 0.05, 0.0)
    for d in range(2):
        stack = gram_all[d].reshape(384, 128) * scale
        corner = stack[128:256, :]
        a_ref[d, 0:128, 0:128] = stack[0:128, :] + ridge
        a_ref[d, 128:256, 0:128] = corner
        a_ref[d, 0:128, 128:256] = corner.T
        a_ref[d, 128:256, 128:256] = stack[256:384, :] + ridge
    steps = terms // STEP
    eliminate(a_ref, e_ref, r_ref, 0, 1)

    @pl.loop(1, scens)
    def _(d):
        arrived(x_in.at[scen_peer(d)], xr_r.at[scen_peer(d)])

    x_sum[...] = lax.fori_loop(1, scens, lambda d, carry: carry + x_in[scen_peer(d)], mom_acc[s])
    own_part = CHUNK // seats
    for j in range(seats):
        seat_out[j] = x_sum[j * own_part : (j + 1) * own_part, :]

    @pl.loop(1, seats)
    def _(d):
        seat_copy(seat_peer(d)).start()

    eliminate(a_ref, e_ref, r_ref, 1, 3)

    arrived(seat_in.at[pl.ds(0, seats - 1)], sr_r)

    seat_all[seat] = lax.fori_loop(
        1, seats, lambda d, carry: carry + seat_in[seat_peer(d)], seat_out[seat]
    )

    @pl.loop(1, seats)
    def _(d):
        seat_all_copy(seat_peer(d)).start()

    eliminate(a_ref, e_ref, r_ref, 3, 5)

    arrived(seat_all.at[pl.ds(0, seats - 1)], sa_r)

    for j in range(seats):
        full[core, s, j * own_part : (j + 1) * own_part, :] = seat_all[j]

    @pl.loop(1, scens)
    def _(d):
        full_copy(scen_peer(d)).start()

    forward_copy(s).start()
    eliminate(a_ref, e_ref, r_ref, 5, 8)

    arrived(rhs_in.at[pl.ds(0, path_devices - 1)], rhs_r)

    def add_rhs(d, carry):
        return carry + rhs_in[path_peer(d)]

    rhs = lax.fori_loop(1, path_devices, add_rhs, rhs_own[...]) * scale
    coef = -jnp.dot(
        jnp.broadcast_to(rhs, (8, terms)), a_ref[1], precision=HI, preferred_element_type=F32
    )[0:1]
    coef_out[1:2, :] = coef
    continuation = add_rows(nn(three_rows(coef), design[1]))
    payoff = surrender[dates[1]]
    values = disc[1] * terminal[...]
    values = jnp.where(mask[1:2, :] > 0, jnp.maximum(payoff, continuation), values)
    values = disc[0] * values
    weighted = design[0] * mask[0:1, :].astype(F32).astype(BF16)
    rhs0_own[...] = add_rows(nt(three_rows(values), weighted))

    @pl.loop(1, path_devices)
    def _(d):
        rhs0_copy(path_peer(d)).start()

    for out, first in ((left3, 0), (right3, 4)):
        out[80:PAIRS, :] = jnp.zeros((PAIRS - 80, paths), F32)
        levels = [
            [one, early[first + v : first + v + 1, :], h[first + v : first + v + 1, :]]
            for v in range(4)
        ]
        products(levels, pair_a, pair_b, out, 3)
    prow = lax.broadcasted_iota(jnp.int32, (PAIRS, 1), 0)
    plane = lax.broadcasted_iota(jnp.int32, (1, SIDE), 1)
    for v, (three, five_) in enumerate(((27, 125), (9, 25), (3, 5), (1, 1))):
        b = jnp.where(prow < 81, (prow // three) % 3, -9)
        m = jnp.where(plane < 625, (plane // five_) % 5, -20)
        b, m = jnp.broadcast_to(b, (PAIRS, SIDE)), jnp.broadcast_to(m, (PAIRS, SIDE))
        ones = ((b == 0) & (m == 1)) | ((b == 1) & ((m == 0) | (m == 2))) | ((b == 2) & (m == 3))
        pattern[v, 0] = jnp.where(m == b, 1.0, 0.0).astype(BF16)
        pattern[v, 1] = jnp.where(ones, 1.0, 0.0).astype(BF16)
        pattern[v, 2] = jnp.where(m == b + 2, 1.0, 0.0).astype(BF16)

    own_tile.wait()

    @pl.loop(0, rows)
    def _(r):
        def pattern_of(first):
            result = None
            for v in range(4):
                block = pattern[v, mine[first + v, first_own + r]]
                result = block if result is None else result * block
            return result

        pick_l[r] = pattern_of(0)
        pick_r[r] = pattern_of(4)

    arrived(gram_in.at[pl.ds(0, seats - 1)], g_s)
    arrived(gram_in.at[pl.ds(0, seats - 1)], ga_s)
    arrived(gram_all.at[core], gf_s)
    arrived(rhs_in.at[pl.ds(0, path_devices - 1)], rhs_s)

    arrived(seat_in.at[pl.ds(0, seats - 1)], sr_s)
    arrived(seat_in.at[pl.ds(0, seats - 1)], sa_s)

    @pl.loop(1, scens)
    def _(d):
        x_copy(scen_peer(d)).wait_send()

    @pl.loop(0, scens)
    def _(t):
        half_copy(t).wait_send()

    @pl.loop(1, scens)
    def _(d):
        t = scen_peer(d)
        arrived(full.at[core, t], xa_r.at[t])
        forward_copy(t).start()

    arrived(rhs0_in.at[pl.ds(0, path_devices - 1)], rhs0_r)
    arrived(rhs0_in.at[pl.ds(0, path_devices - 1)], rhs0_s)

    def add_rhs0(d, carry):
        return carry + rhs0_in[path_peer(d)]

    rhs = lax.fori_loop(1, path_devices, add_rhs0, rhs0_own[...]) * scale
    coef = -jnp.dot(
        jnp.broadcast_to(rhs, (8, terms)), a_ref[0], precision=HI, preferred_element_type=F32
    )[0:1]
    coef_out[0:1, :] = coef
    continuation = add_rows(nn(three_rows(coef), design[0]))
    payoff = surrender[dates[0]]
    final = jnp.where(mask[0:1, :] > 0, jnp.maximum(payoff, continuation), values)
    values_out[...] = final

    rounded = final.astype(BF16).astype(F32)
    lh, ll = halves(left3[...] * rounded)
    rh, rl = halves(right3[...])
    wh, wl = halves(nt(rh, lh) + nt(rh, ll) + nt(rl, lh))
    hot = low[0:PAIRS, :]
    picked = jnp.sum((nn(wh, hot) + nn(wl, hot)) * high[...], axis=0, keepdims=True)
    for t in range(parts.shape[0]):
        for q in range(parts.shape[1]):
            k = (t * parts.shape[1] + q) * 128
            parts[t, q] = picked[:, k : k + 128]

    @pl.loop(1, path_devices)
    def _(d):
        part_copy(path_peer(d)).start()

    @pl.loop(0, scens)
    def _(t):
        arrived(full.at[1 - core, t], fw_r.at[t])

    for k in range(SIDE // 128):
        low_row = k * SIDE
        while low_row < (k + 1) * SIDE:
            c = low_row // CHUNK
            top_row = min((k + 1) * SIDE, (c + 1) * CHUNK)
            whole[low_row - k * SIDE : top_row - k * SIDE, k * 128 : (k + 1) * 128] = full[
                c // scens, c % scens, low_row - c * CHUNK : top_row - c * CHUNK, :
            ]
            low_row = top_row
    mh, ml = halves(whole[...])
    picks = pick_l[...].reshape(rows * PAIRS, SIDE)
    yh, yl = halves(nn(picks, mh) + nn(picks, ml))
    y_high[...] = yh.reshape(y_high.shape)
    y_low[...] = yl.reshape(y_low.shape)

    def second_product(r):
        zh, zl = halves(nt(pick_r[r], y_high[r]) + nt(pick_r[r], y_low[r]))
        z_pack[r, :, 0:PAIRS] = zh
        z_pack[r, :, 128 : 128 + PAIRS] = zl

    z_pack[...] = jnp.zeros(z_pack.shape, BF16)
    pl.loop(0, rows // 2)(second_product)

    arrived(parts_in.at[pl.ds(0, path_devices - 1)], pa_r)

    def add_part(d, carry):
        return carry + parts_in[path_peer(d)]

    mine_part[...] = lax.fori_loop(1, path_devices, add_part, parts[:, p // 8])

    @pl.loop(1, scens)
    def _(d):
        mine_copy(scen_peer(d)).start()

    pl.loop(rows // 2, rows)(second_product)

    column = None
    for v in range(8):
        factor = jnp.where(table[v : v + 1, :] == 2, ROOT_HALF, 1.0)
        column = factor if column is None else column * factor

    @pl.loop(0, rows // 8)
    def _(block):
        lines = []
        for k in range(8):
            r = block * 8 + k
            own = own_scale
            for v in range(8):
                own = own * jnp.where(mine[v, first_own + r] == 2, ROOT_HALF, 1.0)
            picked = nn(z_pack[r], low[...]) * high[...]
            lines.append(jnp.sum(picked, axis=0, keepdims=True) * (column * own))
        gram_out[pl.ds(pl.multiple_of(block * 8, 8), 8), :] = jnp.concatenate(lines, axis=0)

    @pl.loop(1, scens)
    def _(d):
        arrived(mine_in.at[scen_peer(d)], pb_r.at[scen_peer(d)])

    def add_mine(d, carry):
        return carry + mine_in[scen_peer(d)]

    last = lax.fori_loop(1, scens, add_mine, mine_part[s])
    last = pltpu.roll(jnp.broadcast_to(last, (8, 128)), (128 - rows * (p % 8)) % 128, 1)
    rhs_out[...] = last[0:1] * own_scale

    arrived(parts_in.at[pl.ds(0, path_devices - 1)], pa_s)

    @pl.loop(1, scens)
    def _(d):
        t = scen_peer(d)
        full_copy(t).wait_send()
        mine_copy(t).wait_send()

    @pl.loop(0, scens)
    def _(t):
        forward_copy(t).wait_send()


def finish_kernel(values, coef, gram, rhs, values_out, coef_out, gram_out, rhs_out):
    values_out[...] = values[...]
    coef_out[...] = coef[...]
    gram_out[...] = gram[...]
    rhs_out[...] = rhs[:, 0 : rhs_out.shape[1]]


VMEM = pl.BlockSpec(memory_space=pltpu.VMEM)
SMEM = pl.BlockSpec(memory_space=pltpu.SMEM)
DMA = pltpu.SemaphoreType.DMA


def on_device(
    states, exercise_dates, itm_mask, surrender, terminal, discount, ls_table, proxy_table
):
    scens, path_devices = lax.axis_size("scen"), lax.axis_size("path")
    paths = states.shape[3]
    terms, proxy_terms = ls_table.shape[0], proxy_table.shape[0]
    devices = scens * path_devices
    seats = path_devices // 2
    own_rows = proxy_terms // devices
    columns = proxy_table.T
    rows = 384 // seats
    buffer = pltpu.VMEM
    tiles = proxy_terms // 128

    values, coefficients, proxy_gram, proxy_rhs = pl.pallas_call(
        functools.partial(step_kernel, path_devices, scens),
        out_shape=(
            jax.ShapeDtypeStruct((1, paths), F32),
            jax.ShapeDtypeStruct((2, terms), F32),
            jax.ShapeDtypeStruct((own_rows, proxy_terms), F32),
            jax.ShapeDtypeStruct((1, 128), F32),
        ),
        in_specs=[SMEM] * 2 + [pl.BlockSpec(memory_space=pl.ANY)] + [VMEM] * 6,
        out_specs=[VMEM] * 4,
        scratch_shapes=[
            buffer((32, paths), F32), buffer((32, paths), F32),
            buffer((SIDE, paths), F32), buffer((SIDE, paths), F32),
            buffer((SIDE, SIDE), F32),
            buffer((2, terms, paths), BF16),
            buffer((2, seats, rows, 128), F32),
            buffer((seats, rows, 128), F32), buffer((seats, rows, 128), F32), buffer((seats, rows, 128), F32),
            buffer((2, seats, rows, 128), F32),
            buffer((1, terms), F32), buffer((path_devices, 1, terms), F32),
            buffer((1, terms), F32), buffer((path_devices, 1, terms), F32),
            buffer((2, terms, terms), F32), buffer((8, 8, 128), F32), buffer((8, 128), F32),
            buffer((2, scens, CHUNK, 128), F32),
            buffer((scens, CHUNK, 128), F32), buffer((scens, CHUNK, 128), F32), buffer((scens, CHUNK, 128), F32),
            buffer((CHUNK, 128), F32),
            buffer((seats, CHUNK // seats, 128), F32), buffer((seats, CHUNK // seats, 128), F32),
            buffer((seats, CHUNK // seats, 128), F32),
            buffer((2, scens, CHUNK, 128), F32),
            buffer((terms, 8), jnp.int32),
            pltpu.SMEM((8, 128), jnp.int32),
            buffer((4, 3, PAIRS, SIDE), BF16),
            buffer((own_rows, PAIRS, SIDE), BF16), buffer((own_rows, PAIRS, SIDE), BF16),
            buffer((own_rows, PAIRS, SIDE), BF16), buffer((own_rows, PAIRS, SIDE), BF16),
            buffer((own_rows, PAIRS, 256), BF16),
            buffer((256, proxy_terms), BF16), buffer((PAIRS, proxy_terms), F32),
            buffer((PAIRS, paths), F32), buffer((PAIRS, paths), F32),
            buffer((scens, tiles // scens, 1, 128), F32),
            buffer((path_devices, scens, 1, 128), F32),
            buffer((scens, 1, 128), F32), buffer((scens, 1, 128), F32),
            DMA, DMA,
            DMA, DMA, DMA, DMA, DMA, DMA,
            DMA, DMA, DMA, DMA,
            DMA((scens,)), DMA((scens,)),
            DMA((scens,)), DMA((scens,)), DMA, DMA, DMA, DMA,
            DMA((scens,)), DMA((scens,)), DMA((scens,)), DMA((scens,)),
            DMA, DMA,
            DMA((scens,)), DMA((scens,)), DMA,
        ],
        compiler_params=pltpu.CompilerParams(collective_id=0, has_side_effects=True),
        name="step",
    )(
        exercise_dates[0], discount[0], columns, states[0], itm_mask[0], surrender.transpose(1, 0, 2), terminal,
        ls_table.T, columns,
    )
    values, coefficients, proxy_gram, proxy_rhs = pl.pallas_call(
        finish_kernel,
        out_shape=(
            jax.ShapeDtypeStruct((1, paths), F32),
            jax.ShapeDtypeStruct((2, terms), F32),
            jax.ShapeDtypeStruct((own_rows, proxy_terms), F32),
            jax.ShapeDtypeStruct((1, own_rows), F32),
        ),
        in_specs=[VMEM] * 4,
        out_specs=[VMEM] * 4,
        name="finish",
    )(values, coefficients, proxy_gram, proxy_rhs)
    return (values, coefficients[None], proxy_gram, proxy_rhs[0])


def solution(mesh):
    placed = (
        P("scen", None, None, "path"),
        P("scen", None),
        P("scen", None, "path"),
        P("scen", None, "path"),
        P("scen", "path"),
        P("scen", None),
        P(),
        P(),
    )
    return jax.shard_map(
        on_device,
        mesh=mesh,
        in_specs=placed,
        out_specs=(
            P("scen", "path"),
            P("scen", None, None),
            P(("scen", "path"), None),
            P(("scen", "path")),
        ),
        check_vma=False,
    )
```
